512 devices in a mesh: space: 32 (over z, x), vel: 16 (over y, core).
Axes of the slice: x: 4, y: 8, z: 8, core: 2. Of those that a mesh axis runs over, the one named last changes fastest.
Arguments:
- dist: bfloat16 [512, 64, 4096], P('space', None, 'vel'), may hold values from -6 to 6
- send_faces: int32 [32, 2, 16], P('space'), may hold values from 0 to 95
- send_count: int32 [32, 2], P('space'), may hold values from 1 to 16, as said below
- source_face: int32 [512, 6], P('space'), may hold values from 0 to 127, as said below
- subface: int32 [512, 6], P('space'), may hold values from 0 to 4
- alpha: float32 [4, 4096], replicated, may hold values from -1 to 1
- beta: float32 [5, 4096], replicated, may hold values from -1 to 1
Outputs:
- relaxed: bfloat16 [512, 64, 4096], P('space', None, 'vel')
The draws below stay inside these ranges and needn't reach their ends.
Inputs may be any that keep to these rules, and one draw needn't show every extreme that they name: `source_face`: for each face of a block: below 96 a local face of the same block; from 96 the 16 slots of the previous block's block toward the next one, then the 16 slots of the next block's block toward the previous one. Every slot of these two blocks is read by exactly one face of the block. `send_count`: for each direction some block's padded trace block is full. `send_faces`: local face numbers, element times 6 plus face.
All inputs are finite; a program needn't handle non-finite values.
Results may differ from the reference program's by a relative error of at most 0.0057.
Values may be sent and summed in bfloat16 or wider, within the bound.
No kernel may reach another device: no remote copies, remote signals or barrier semaphores. Data moves between devices by JAX's collectives and lax.ppermute only.
A program may use at most 64 MiB of HBM per device.

```python
import jax
import jax.numpy as jnp
import numpy as np
from jax import lax

E_DEV = 16
NODES = 64
VSIDE = 16
MODES = 4
ELEMS = 512
VEL = 4096
MAXB = 16
N_SPACE = 32


def draw_source_face(key, part):
    faces = 6 * E_DEV
    blocks = ELEMS // E_DEV

    def one_block(block_key):
        order = jax.random.permutation(block_key, faces)
        local = jax.random.randint(jax.random.fold_in(block_key, 1), (faces,), 0, faces)
        remote = faces + jnp.arange(2 * MAXB)
        return local.at[order[:2 * MAXB]].set(remote).reshape(E_DEV, 6)
    keys = jax.random.split(jax.random.fold_in(key, 11), blocks)
    return jax.vmap(one_block)(keys).reshape(ELEMS, 6).astype(jnp.int32)


def draw_send_count(key, part):
    blocks = ELEMS // E_DEV
    counts = jax.random.randint(jax.random.fold_in(key, 23), (blocks, 2), 1, MAXB + 1)
    chosen = jax.random.randint(jax.random.fold_in(key, 29), (2,), 0, blocks)
    return counts.at[chosen, jnp.arange(2)].set(MAXB).astype(jnp.int32)


def touch_ends(values, stream_key, least, largest):
    shape = values.shape
    spot = [jax.random.randint(jax.random.fold_in(stream_key, axis), (), 0, shape[axis]) for axis in range(len(shape))]
    values = values.at[tuple(spot)].set(least)
    longest = shape.index(max(shape))
    spot[longest] = (spot[longest] + 1) % shape[longest]
    return values.at[tuple(spot)].set(largest)


def shard_levels(key, shape, cuts, low, largest):
    level, own = 1.0, jax.random.fold_in(key, 6)
    for position, parts in cuts:
        heights = jnp.exp(jax.random.uniform(jax.random.fold_in(own, position), (parts,), jnp.float32, low / len(cuts), largest / len(cuts)))
        level = level * jnp.repeat(heights, shape[position] // parts).reshape([-1 if axis == position else 1 for axis in range(len(shape))])
    return level


def centred(key, dims, width, most, pieces=(), kind=jnp.bfloat16):
    loudness = shard_levels(key, dims, pieces, -0.22, 0.18) if pieces else 1.0
    entries = jax.random.normal(key, dims, jnp.float32) * width * loudness
    return jnp.minimum(jnp.maximum(entries, -most), most).astype(kind)


def setup_inputs(seed: int = 0) -> dict:
    seeds = jax.random.split(jax.random.key(seed), 8)
    return {
        "dist": centred(seeds[0], (ELEMS, NODES, VEL), 1.0, 6.0, ((0, 32), (2, 16))),
        "send_faces": touch_ends(jax.random.randint(seeds[1], (N_SPACE, 2, MAXB), 0, 6 * E_DEV), jax.random.fold_in(seeds[1], 1), 0, (6 * E_DEV) - 1).astype(jnp.int32),
        "send_count": draw_send_count(jax.random.fold_in(seeds[7], 71), 0),
        "source_face": draw_source_face(jax.random.fold_in(seeds[7], 71), 0),
        "subface": touch_ends(jax.random.randint(seeds[4], (ELEMS, 6), 0, 5), jax.random.fold_in(seeds[4], 1), 0, 4).astype(jnp.int32),
        "alpha": jnp.clip(jax.random.uniform(seeds[5], (MODES, VEL), jnp.float32, -1.0, 1.0), -1.0, 1.0),
        "beta": jnp.clip(jax.random.uniform(seeds[6], (MODES + 1, VEL), jnp.float32, -1.0, 1.0), -1.0, 1.0),
    }


courant = 0.1
lift_weight = 6.0
relax_step = 0.5
highest = lax.Precision.HIGHEST

def lobatto_points():
    return np.array([-1.0, -1.0 / np.sqrt(5.0), 1.0 / np.sqrt(5.0), 1.0])

def lagrange_table(targets):
    points = lobatto_points()
    result = np.ones((targets.shape[0], 4))
    for column in range(4):
        for second in range(4):
            if second != column:
                result[:, column] = result[:, column] * (targets - points[second]) / (points[column] - points[second])
    return result

def derivative_table():
    points = lobatto_points()
    result = np.zeros((4, 4))
    for row_at in range(4):
        for column in range(4):
            total = 0.0
            for skipped in range(4):
                if skipped != column:
                    factor = 1.0 / (points[column] - points[skipped])
                    for second in range(4):
                        if second != column and second != skipped:
                            factor = factor * (points[row_at] - points[second]) / (points[column] - points[second])
                    total = total + factor
            result[row_at, column] = total
    return result

def cosine_table():
    index_list = np.arange(VSIDE)
    result = np.sqrt(2.0 / VSIDE) * np.cos(np.pi * (index_list[None, :] + 0.5) * index_list[:, None] / VSIDE)
    result[0] = result[0] / np.sqrt(2.0)
    return result

def static_tables():
    derivative = derivative_table()
    eye_four = np.eye(4)
    gradients = np.stack([np.kron(np.kron(derivative, eye_four), eye_four), np.kron(np.kron(eye_four, derivative), eye_four), np.kron(np.kron(eye_four, eye_four), derivative)])
    selector = np.zeros((96, 64))
    for axis_at in range(3):
        for side_at in range(2):
            filled = 0
            for node_at in range(64):
                digits = (node_at // 16, node_at // 4 % 4, node_at % 4)
                if digits[axis_at] == 3 * side_at:
                    selector[(2 * axis_at + side_at) * 16 + filled, node_at] = 1.0
                    filled = filled + 1
    points = lobatto_points()
    halves = [lagrange_table((points - 1.0) / 2.0), lagrange_table((points + 1.0) / 2.0)]
    mortar = np.stack([np.eye(16)] + [np.kron(halves[(which - 1) // 2], halves[(which - 1) % 2]) for which in range(1, 5)])
    return (gradients, selector, mortar)

def velocity_components(first, count):
    index_list = first + jnp.arange(count)
    along = [index_list // (VSIDE * VSIDE), index_list // VSIDE % VSIDE, index_list % VSIDE]
    return jnp.stack([(entry.astype(jnp.float32) + 0.5) * (2.0 / VSIDE) - 1.0 for entry in along])

def outgoing_blocks(block, sends, counts, selector):
    faces = jnp.einsum('tn,env->etv', selector, block.astype(jnp.float32)).astype(jnp.bfloat16)
    rows = faces.reshape(E_DEV * 6, 16, VEL)
    picked = rows[sends.reshape(-1)].reshape(2, MAXB, 16, VEL)
    live = jnp.arange(MAXB)[None, :] < counts[:, None]
    return jnp.where(live[:, :, None, None], picked, jnp.zeros_like(picked))

def transport(block, from_prev, from_next, sources, levels, tables, speeds):
    gradients, selector, mortar = tables
    values = block.astype(jnp.float32)
    rows = jnp.einsum('tn,env->etv', selector, values).astype(jnp.bfloat16).reshape(E_DEV * 6, 16, VEL)
    drift = jnp.zeros_like(values)
    for axis_at in range(3):
        drift = drift + speeds[axis_at] * jnp.einsum('nm,emv->env', gradients[axis_at], values)
    table = jnp.concatenate([rows, from_prev, from_next], axis=0)
    neighbour = table[sources.reshape(-1)].astype(jnp.float32)
    projected = jnp.einsum('ftu,fuv->ftv', mortar[levels.reshape(-1)], neighbour)
    inflow = jnp.minimum(jnp.stack([-speeds[0], speeds[0], -speeds[1], speeds[1], -speeds[2], speeds[2]]), 0.0)
    jump = (rows.astype(jnp.float32) - projected).reshape(E_DEV, 6, 16, VEL) * inflow[None, :, None, :]
    lifted = jnp.einsum('tn,etv->env', selector, jump.reshape(E_DEV, 96, VEL), precision=highest)
    return (values - courant * drift + courant * lift_weight * lifted).astype(jnp.bfloat16)

def collide_element(element, kernels, cosine):
    values = element.astype(jnp.float32)
    cube = values.reshape(NODES, VSIDE, VSIDE, VSIDE)
    spectrum = jnp.einsum('ai,nijk->najk', cosine, cube, precision=highest)
    spectrum = jnp.einsum('bj,najk->nabk', cosine, spectrum, precision=highest)
    spectrum = jnp.einsum('ck,nabk->nabc', cosine, spectrum, precision=highest)
    filtered = spectrum[:, None] * kernels[None]
    fields = jnp.einsum('ai,nmabc->nmibc', cosine, filtered, precision=highest)
    fields = jnp.einsum('bj,nmibc->nmijc', cosine, fields, precision=highest)
    fields = jnp.einsum('ck,nmijc->nmijk', cosine, fields, precision=highest).reshape(NODES, 2 * MODES + 1, VEL)
    gain = lax.optimization_barrier(jnp.sum(fields[:, :MODES] * fields[:, MODES:2 * MODES], axis=1))
    loss = values * fields[:, 2 * MODES]
    return (values + relax_step * (gain - loss)).astype(jnp.bfloat16)

def reference(dist, send_faces, send_count, source_face, subface, alpha, beta):
    gradients, selector, mortar = static_tables()
    tables = (jnp.asarray(gradients, jnp.bfloat16).astype(jnp.float32), jnp.asarray(selector, jnp.float32), jnp.asarray(mortar, jnp.bfloat16).astype(jnp.float32))
    speeds = velocity_components(0, VEL)
    blocks = dist.reshape(N_SPACE, E_DEV, NODES, VEL)

    def send_step(item):
        return outgoing_blocks(item[0], item[1], item[2], tables[1])
    outgoing = lax.map(send_step, (blocks, send_faces, send_count))
    from_prev = jnp.roll(outgoing[:, 1], 1, axis=0)
    from_next = jnp.roll(outgoing[:, 0], -1, axis=0)

    def move_step(item):
        return transport(item[0], item[1], item[2], item[3], item[4], tables, speeds)
    updated = lax.map(move_step, (blocks, from_prev, from_next, source_face.reshape(N_SPACE, E_DEV, 6), subface.reshape(N_SPACE, E_DEV, 6)))
    cosine = jnp.asarray(cosine_table(), jnp.float32)
    kernels = jnp.concatenate([alpha, beta], axis=0).reshape(2 * MODES + 1, VSIDE, VSIDE, VSIDE)

    def collide_step(element):
        return collide_element(element, kernels, cosine)
    return lax.map(collide_step, updated.reshape(ELEMS, NODES, VEL))
```

```python
import jax
import jax.numpy as jnp
import ml_dtypes
import numpy as np
from jax import lax
from jax.experimental import pallas as pl
from jax.experimental.pallas import tpu as pltpu
from jax.sharding import PartitionSpec as P

VSIDE = 16
SLOTS = 16
GROUP = 16


courant = 0.1
lift_weight = 6.0
relax_step = 0.5


def passed_along(block, axis, distance):
    devices = range(lax.axis_size(axis))
    route = [((i - distance) % len(devices), i) for i in devices]
    return lax.ppermute(block, axis, route)


def lobatto_points():
    return np.array([-1.0, -1.0 / np.sqrt(5.0), 1.0 / np.sqrt(5.0), 1.0])


def lagrange_table(targets):
    points = lobatto_points()
    result = np.ones((targets.shape[0], 4))
    for column in range(4):
        for second in range(4):
            if second != column:
                result[:, column] = (
                    result[:, column]
                    * (targets - points[second])
                    / (points[column] - points[second])
                )
    return result


def derivative_table():
    points = lobatto_points()
    result = np.zeros((4, 4))
    for row_at in range(4):
        for column in range(4):
            total = 0.0
            for skipped in range(4):
                if skipped != column:
                    factor = 1.0 / (points[column] - points[skipped])
                    for second in range(4):
                        if second != column and second != skipped:
                            factor = (
                                factor
                                * (points[row_at] - points[second])
                                / (points[column] - points[second])
                            )
                    total = total + factor
            result[row_at, column] = total
    return result


def cosine_table():
    index_list = np.arange(VSIDE)
    result = np.sqrt(2.0 / VSIDE) * np.cos(
        np.pi * (index_list[None, :] + 0.5) * index_list[:, None] / VSIDE
    )
    result[0] = result[0] / np.sqrt(2.0)
    return result


def static_tables():
    derivative = derivative_table()
    eye_four = np.eye(4)
    gradients = np.stack(
        [
            np.kron(np.kron(derivative, eye_four), eye_four),
            np.kron(np.kron(eye_four, derivative), eye_four),
            np.kron(np.kron(eye_four, eye_four), derivative),
        ]
    )
    selector = np.zeros((96, 64))
    for axis_at in range(3):
        for side_at in range(2):
            filled = 0
            for node_at in range(64):
                digits = (node_at // 16, node_at // 4 % 4, node_at % 4)
                if digits[axis_at] == 3 * side_at:
                    selector[(2 * axis_at + side_at) * 16 + filled, node_at] = 1.0
                    filled = filled + 1
    points = lobatto_points()
    halves = [lagrange_table((points - 1.0) / 2.0), lagrange_table((points + 1.0) / 2.0)]
    mortar = np.stack(
        [np.eye(16)]
        + [np.kron(halves[(which - 1) // 2], halves[(which - 1) % 2]) for which in range(1, 5)]
    )
    return (gradients, selector, mortar)


def velocity_components(first, count):
    index_list = first + jnp.arange(count)
    along = [index_list // (VSIDE * VSIDE), index_list // VSIDE % VSIDE, index_list % VSIDE]
    return jnp.stack([(entry.astype(jnp.float32) + 0.5) * (2.0 / VSIDE) - 1.0 for entry in along])


def split_table(table):
    high = np.asarray(table, np.float32).astype(ml_dtypes.bfloat16)
    rest = np.asarray(table, np.float64) - high.astype(np.float64)
    return (high, np.asarray(rest, np.float32).astype(ml_dtypes.bfloat16))


def transport_tables():
    gradients, selector, mortar = static_tables()
    low = mortar.astype(np.float32).astype(ml_dtypes.bfloat16).astype(np.float64)
    tables = np.zeros((6, 5, 64, 256))
    for face in range(6):
        lift = selector[face * 16 : face * 16 + 16].T
        sign = -1.0 if face % 2 == 0 else 1.0
        for level in range(5):
            spread = sign * (lift @ low[level])
            tables[face, level, :, 64 + face * 16 : 80 + face * 16] = 4.0 * spread
            tables[face, level, :, 160 + face * 16 : 176 + face * 16] = 2.0 * spread
            if face % 2 == 0:
                tables[face, level, :, :64] = gradients[face // 2]
    return tables.astype(np.float32).astype(ml_dtypes.bfloat16)


def cosine_forward(values):
    count = len(values)
    if count == 1:
        return values
    half = count // 2
    sums = [values[i] + values[count - 1 - i] for i in range(half)]
    gaps = [
        (values[i] - values[count - 1 - i]) * float(0.5 / np.cos((i + 0.5) * np.pi / count))
        for i in range(half)
    ]
    even, odd = cosine_forward(sums), cosine_forward(gaps)
    result = []
    for i in range(half):
        result.append(even[i])
        result.append(odd[i] + odd[i + 1] if i + 1 < half else odd[i])
    return result


def cosine_backward(values):
    count = len(values)
    if count == 1:
        return values
    half = count // 2
    even = [values[2 * i] for i in range(half)]
    odd = [values[1]] + [values[2 * i - 1] + values[2 * i + 1] for i in range(1, half)]
    sums, gaps = cosine_backward(even), cosine_backward(odd)
    scaled = [gaps[i] * float(0.5 / np.cos((i + 0.5) * np.pi / count)) for i in range(half)]
    return [sums[i] + scaled[i] for i in range(half)] + [
        sums[half - 1 - i] - scaled[half - 1 - i] for i in range(half)
    ]


def dot(left, right):
    return jnp.dot(left, right, preferred_element_type=jnp.float32)


def send_kernel(faces_ref, count_ref, dist_ref, select_ref, back_ref, ahead_ref, rows):
    elements = dist_ref.shape[0]
    for at in range(elements):
        traces = dot(select_ref[...], dist_ref[at]).astype(jnp.bfloat16)
        rows[6 * at : 6 * at + 6] = traces.reshape(6, 16, dist_ref.shape[2])
    for way, out in enumerate((back_ref, ahead_ref)):
        for slot in range(SLOTS):
            trace = rows[faces_ref[way * SLOTS + slot]]
            keep = jnp.where(slot < count_ref[way], 1.0, 0.0).astype(jnp.bfloat16)
            out[slot] = trace * keep


def move_kernel(
    source_ref,
    level_ref,
    dist_ref,
    prev_ref,
    next_ref,
    select_ref,
    table_ref,
    mask_ref,
    speed_ref,
    keep_ref,
    out_ref,
    rows,
    stack,
):
    elements = dist_ref.shape[0]
    faces = 6 * elements
    for at in range(elements):
        traces = dot(select_ref[...], dist_ref[at]).astype(jnp.bfloat16)
        rows[6 * at : 6 * at + 6] = traces.reshape(6, 16, dist_ref.shape[2])
    rows[faces : faces + SLOTS] = prev_ref[...]
    rows[faces + SLOTS : faces + 2 * SLOTS] = next_ref[...]
    for at in range(elements):
        stack[at, :64] = dist_ref[at]
        for face in range(6):
            trace = rows[source_ref[6 * at + face]] * mask_ref[face]
            stack[at, 64 + 16 * face : 80 + 16 * face] = trace
            stack[at, 160 + 16 * face : 176 + 16 * face] = trace
        left = jnp.concatenate(
            [
                table_ref[2 * axis, level_ref[6 * at + 2 * axis]]
                + table_ref[2 * axis + 1, level_ref[6 * at + 2 * axis + 1]]
                for axis in range(3)
            ],
            axis=0,
        )
        moved = dot(left, stack[at])
        total = dist_ref[at].astype(jnp.float32) * keep_ref[...]
        for axis in range(3):
            total = total + moved[64 * axis : 64 * axis + 64] * speed_ref[axis : axis + 1, :]
        out_ref[at] = total.astype(jnp.bfloat16)


def collide_kernel(dist_ref, kern_ref, into_ref, back_ref, out_ref):
    nodes, plane = dist_ref.shape[1], dist_ref.shape[2]

    def planes(array):
        cube = array.reshape(VSIDE, nodes, plane)
        return [cube[i] for i in range(VSIDE)]

    values = dist_ref[...].reshape(VSIDE * nodes, plane)
    spectrum = cosine_forward(planes(dot(values, into_ref[0]) + dot(values, into_ref[1])))

    def field(which):
        filtered = jnp.concatenate(
            [
                (spectrum[i] * kern_ref[which, i : i + 1, :]).astype(jnp.bfloat16)
                for i in range(VSIDE)
            ],
            axis=0,
        )
        return cosine_backward(planes(dot(filtered, back_ref[0]) + dot(filtered, back_ref[1])))

    modes = (kern_ref.shape[0] - 1) // 2
    gain = None
    for mode in range(modes):
        first, second = field(mode), field(modes + mode)
        products = [a * b for a, b in zip(first, second)]
        gain = products if gain is None else [a + b for a, b in zip(gain, products)]
    loss = field(2 * modes)
    for i in range(VSIDE):
        value = dist_ref[i].astype(jnp.float32)
        out_ref[i] = (value + relax_step * (gain[i] - value * loss[i])).astype(jnp.bfloat16)


def in_vmem():
    return pl.BlockSpec(memory_space=pltpu.VMEM)


def in_smem():
    return pl.BlockSpec(memory_space=pltpu.SMEM)


def on_device(dist, send_faces, send_count, source_face, subface, alpha, beta):
    elements, nodes, vel_local = dist.shape
    faces = 6 * elements
    _, selector, _ = static_tables()
    select_low = jnp.asarray(selector, jnp.bfloat16)
    speeds = velocity_components(lax.axis_index("vel") * vel_local, vel_local)
    trace_shape = jax.ShapeDtypeStruct((SLOTS, 16, vel_local), jnp.bfloat16)

    back, ahead = pl.pallas_call(
        send_kernel,
        out_shape=(trace_shape, trace_shape),
        in_specs=[in_smem(), in_smem(), in_vmem(), in_vmem()],
        out_specs=(in_vmem(), in_vmem()),
        scratch_shapes=[pltpu.VMEM((faces, 16, vel_local), jnp.bfloat16)],
        name="send_traces",
    )(send_faces.reshape(-1), send_count.reshape(-1), dist, select_low)
    from_prev = passed_along(ahead, "space", 1)
    from_next = passed_along(back, "space", -1)

    on = jnp.stack([m for a in range(3) for m in (speeds[a] > 0.0, speeds[a] < 0.0)])
    masks = jnp.broadcast_to(on[:, None, :], (6, 16, vel_local)).astype(jnp.bfloat16)
    inflow = jnp.where(on, jnp.repeat(jnp.abs(speeds), 2, axis=0), 0.0)
    member = jnp.asarray(selector.reshape(6, 16, 64).sum(axis=1), jnp.float32)
    keep = 1.0 - courant * lift_weight * jnp.sum(member[:, :, None] * inflow[:, None, :], axis=0)
    updated = pl.pallas_call(
        move_kernel,
        out_shape=jax.ShapeDtypeStruct(dist.shape, jnp.bfloat16),
        in_specs=[in_smem(), in_smem()] + [in_vmem()] * 8,
        out_specs=in_vmem(),
        scratch_shapes=[
            pltpu.VMEM((faces + 2 * SLOTS, 16, vel_local), jnp.bfloat16),
            pltpu.VMEM((elements, 256, vel_local), jnp.bfloat16),
        ],
        name="transport",
    )(
        source_face.reshape(-1),
        subface.reshape(-1),
        dist,
        from_prev,
        from_next,
        select_low,
        jnp.asarray(transport_tables()),
        masks,
        -courant * speeds,
        keep,
    )

    plane = VSIDE * VSIDE
    cosine = cosine_table()
    pair = np.kron(cosine, cosine)
    into = jnp.asarray(np.stack(split_table(pair.T)))
    out_of = jnp.asarray(np.stack(split_table(pair)))
    norms = np.full((VSIDE, 1), 2.0 / VSIDE, np.float32)
    norms[0] = 1.0 / VSIDE
    kernels = jnp.concatenate([alpha, beta], axis=0).reshape(-1, VSIDE, plane) * norms
    gathered = lax.all_to_all(updated, "vel", split_axis=0, concat_axis=0, tiled=True)
    block = pl.BlockSpec((VSIDE, GROUP, plane), lambda g: (0, g, 0))
    mixed = pl.pallas_call(
        collide_kernel,
        out_shape=jax.ShapeDtypeStruct(gathered.shape, jnp.bfloat16),
        grid=(nodes // GROUP,),
        in_specs=[
            block,
            pl.BlockSpec(kernels.shape, lambda g: (0, 0, 0)),
            pl.BlockSpec(into.shape, lambda g: (0, 0, 0)),
            pl.BlockSpec(out_of.shape, lambda g: (0, 0, 0)),
        ],
        out_specs=block,
        name="collide",
    )(gathered, kernels, into, out_of)
    return lax.all_to_all(mixed, "vel", split_axis=0, concat_axis=0, tiled=True)


def solution(mesh):
    return jax.shard_map(
        on_device,
        mesh=mesh,
        in_specs=(
            P("space", None, "vel"),
            P("space", None, None),
            P("space", None),
            P("space", None),
            P("space", None),
            P(),
            P(),
        ),
        out_specs=P("space", None, "vel"),
        check_vma=False,
    )
```

```python
import jax
import jax.numpy as jnp
import ml_dtypes
import numpy as np
from jax import lax
from jax.experimental import pallas as pl
from jax.experimental.pallas import tpu as pltpu
from jax.sharding import PartitionSpec as P

VSIDE = 16
SLOTS = 16
GROUP = 16
PIECES = 4


courant = 0.1
lift_weight = 6.0
relax_step = 0.5


def passed_along(block, axis, distance):
    devices = range(lax.axis_size(axis))
    route = [((i - distance) % len(devices), i) for i in devices]
    return lax.ppermute(block, axis, route)


def lobatto_points():
    return np.array([-1.0, -1.0 / np.sqrt(5.0), 1.0 / np.sqrt(5.0), 1.0])


def lagrange_table(targets):
    points = lobatto_points()
    result = np.ones((targets.shape[0], 4))
    for column in range(4):
        for second in range(4):
            if second != column:
                result[:, column] = (
                    result[:, column]
                    * (targets - points[second])
                    / (points[column] - points[second])
                )
    return result


def derivative_table():
    points = lobatto_points()
    result = np.zeros((4, 4))
    for row_at in range(4):
        for column in range(4):
            total = 0.0
            for skipped in range(4):
                if skipped != column:
                    factor = 1.0 / (points[column] - points[skipped])
                    for second in range(4):
                        if second != column and second != skipped:
                            factor = (
                                factor
                                * (points[row_at] - points[second])
                                / (points[column] - points[second])
                            )
                    total = total + factor
            result[row_at, column] = total
    return result


def cosine_table():
    index_list = np.arange(VSIDE)
    result = np.sqrt(2.0 / VSIDE) * np.cos(
        np.pi * (index_list[None, :] + 0.5) * index_list[:, None] / VSIDE
    )
    result[0] = result[0] / np.sqrt(2.0)
    return result


def static_tables():
    derivative = derivative_table()
    eye_four = np.eye(4)
    gradients = np.stack(
        [
            np.kron(np.kron(derivative, eye_four), eye_four),
            np.kron(np.kron(eye_four, derivative), eye_four),
            np.kron(np.kron(eye_four, eye_four), derivative),
        ]
    )
    selector = np.zeros((96, 64))
    for axis_at in range(3):
        for side_at in range(2):
            filled = 0
            for node_at in range(64):
                digits = (node_at // 16, node_at // 4 % 4, node_at % 4)
                if digits[axis_at] == 3 * side_at:
                    selector[(2 * axis_at + side_at) * 16 + filled, node_at] = 1.0
                    filled = filled + 1
    points = lobatto_points()
    halves = [lagrange_table((points - 1.0) / 2.0), lagrange_table((points + 1.0) / 2.0)]
    mortar = np.stack(
        [np.eye(16)]
        + [np.kron(halves[(which - 1) // 2], halves[(which - 1) % 2]) for which in range(1, 5)]
    )
    return (gradients, selector, mortar)


def split_table(table):
    high = np.asarray(table, np.float32).astype(ml_dtypes.bfloat16)
    rest = np.asarray(table, np.float64) - high.astype(np.float64)
    return (high, np.asarray(rest, np.float32).astype(ml_dtypes.bfloat16))


def mortar_lifts():
    _, selector, mortar = static_tables()
    tables = np.zeros((6, 5, 64, 128))
    for face in range(6):
        lift = selector[face * 16 : face * 16 + 16].T
        sign = -1.0 if face % 2 == 0 else 1.0
        for level in range(5):
            tables[face, level, :, face * 16 : face * 16 + 16] = sign * (lift @ mortar[level])
    return tables.astype(np.float32).astype(ml_dtypes.bfloat16)


def cosine_forward(values):
    count = len(values)
    if count == 1:
        return values
    half = count // 2
    sums = [values[i] + values[count - 1 - i] for i in range(half)]
    gaps = [
        (values[i] - values[count - 1 - i]) * float(0.5 / np.cos((i + 0.5) * np.pi / count))
        for i in range(half)
    ]
    even, odd = cosine_forward(sums), cosine_forward(gaps)
    result = []
    for i in range(half):
        result.append(even[i])
        result.append(odd[i] + odd[i + 1] if i + 1 < half else odd[i])
    return result


def cosine_backward(values):
    count = len(values)
    if count == 1:
        return values
    half = count // 2
    even = [values[2 * i] for i in range(half)]
    odd = [values[1]] + [values[2 * i - 1] + values[2 * i + 1] for i in range(1, half)]
    sums, gaps = cosine_backward(even), cosine_backward(odd)
    scaled = [gaps[i] * float(0.5 / np.cos((i + 0.5) * np.pi / count)) for i in range(half)]
    return [sums[i] + scaled[i] for i in range(half)] + [
        sums[half - 1 - i] - scaled[half - 1 - i] for i in range(half)
    ]


def dot(left, right):
    return jnp.dot(left, right, preferred_element_type=jnp.float32)


def face_nodes(face, shape, along):
    at = lax.broadcasted_iota(jnp.int32, shape, along)
    axis, side = face // 2, face % 2
    if axis == 0:
        return at + 48 * side
    high, low = at >> 2, at & 3
    return 16 * high + 12 * side + low if axis == 1 else 16 * high + 4 * low + 3 * side


def local_speeds(shape):
    index = lax.axis_index("vel") * shape[-1] + lax.broadcasted_iota(jnp.int32, shape, len(shape) - 1)
    along = [index // (VSIDE * VSIDE), (index // VSIDE) & (VSIDE - 1), index & (VSIDE - 1)]
    return [(entry.astype(jnp.float32) + 0.5) * (2.0 / VSIDE) - 1.0 for entry in along]


def inflow_faces(speeds):
    return [speeds[f // 2] > 0.0 if f % 2 == 0 else speeds[f // 2] < 0.0 for f in range(6)]


def inflow_masks(shape):
    ones = [jnp.where(on, 1.0, 0.0) for on in inflow_faces(local_speeds(shape))]
    return [one.astype(jnp.bfloat16) for one in ones]


def send_kernel(faces_ref, count_ref, dist_ref, back_ref, ahead_ref, held, rows, sems):
    elements, nodes, width = held.shape
    step = elements // PIECES

    def piece(at):
        part = pl.ds(at * step, step)
        return pltpu.make_async_copy(dist_ref.at[part], held.at[part], sems.at[at])

    for at in range(PIECES):
        piece(at).start()
    node = lax.broadcasted_iota(jnp.int32, (16, nodes), 1)
    select = jnp.concatenate(
        [jnp.where(face_nodes(f, (16, nodes), 0) == node, 1.0, 0.0) for f in range(6)], axis=0
    ).astype(jnp.bfloat16)
    for at in range(elements):
        if at % step == 0:
            piece(at // step).wait()
        traces = dot(select, held[at]).astype(jnp.bfloat16)
        rows[6 * at : 6 * at + 6] = traces.reshape(6, 16, width)
    for way, out in enumerate((back_ref, ahead_ref)):
        for slot in range(SLOTS):
            trace = rows[faces_ref[0, way, slot]]
            keep = jnp.where(slot < count_ref[0, way], 1.0, 0.0).astype(jnp.bfloat16)
            out[slot] = trace * keep


def lift_traces(at, level_ref, lift_ref, stack, total):
    speeds = local_speeds((1, total.shape[-1]))
    left = jnp.concatenate(
        [
            lift_ref[2 * axis, level_ref[2 * axis, at]]
            + lift_ref[2 * axis + 1, level_ref[2 * axis + 1, at]]
            for axis in range(3)
        ],
        axis=0,
    )
    lifted = dot(left, stack[at])
    for axis in range(3):
        weight = -courant * lift_weight * speeds[axis]
        total = total + lifted[64 * axis : 64 * axis + 64] * weight
    return total


def local_kernel(source_ref, level_ref, held, rows, gradient_ref, lift_ref, out_ref, table, stack):
    elements, nodes, width = held.shape
    faces = 6 * elements
    table[:faces] = rows[...]
    table[faces] = jnp.zeros((16, width), jnp.bfloat16)
    speeds = local_speeds((1, width))
    masks = inflow_masks((16, width))
    wide = local_speeds((nodes, width))
    node = lax.broadcasted_iota(jnp.int32, (nodes, width), 0)
    digits = [node >> 4, (node >> 2) & 3, node & 3]
    loss = jnp.zeros((nodes, width), jnp.float32)
    for face, on in enumerate(inflow_faces(wide)):
        member = jnp.logical_and(on, digits[face // 2] == 3 * (face % 2))
        loss = loss + jnp.where(member, jnp.abs(wide[face // 2]), 0.0)
    keep = 1.0 - courant * lift_weight * loss
    for at in range(elements):
        for face in range(6):
            trace = table[jnp.minimum(source_ref[face, at], faces)] * masks[face]
            stack[at, 16 * face : 16 * face + 16] = trace
        stack[at, 96:] = jnp.zeros((32, width), jnp.bfloat16)
        total = held[at].astype(jnp.float32) * keep
        moved = dot(gradient_ref[...], held[at])
        for axis in range(3):
            total = total + moved[64 * axis : 64 * axis + 64] * (-courant * speeds[axis])
        out_ref[at] = lift_traces(at, level_ref, lift_ref, stack, total)


def remote_kernel(source_ref, level_ref, part_ref, prev_ref, next_ref, lift_ref, out_ref, table, stack):
    elements, _, width = part_ref.shape
    faces = 6 * elements
    table[0] = jnp.zeros((16, width), jnp.bfloat16)
    table[1 : SLOTS + 1] = prev_ref[...]
    table[SLOTS + 1 :] = next_ref[...]
    masks = inflow_masks((16, width))
    for at in range(elements):
        for face in range(6):
            trace = table[jnp.maximum(source_ref[face, at] - (faces - 1), 0)] * masks[face]
            stack[at, 16 * face : 16 * face + 16] = trace
        stack[at, 96:] = jnp.zeros((32, width), jnp.bfloat16)
        total = lift_traces(at, level_ref, lift_ref, stack, part_ref[at])
        out_ref[at] = total.astype(jnp.bfloat16)


def collide_kernel(dist_ref, kern_ref, into_ref, back_ref, out_ref, spectrum, fields, first, gain):
    nodes, plane = dist_ref.shape[1], dist_ref.shape[2]
    modes = (kern_ref.shape[0] - 1) // 2
    order = [m for pair in range(modes) for m in (pair, modes + pair)] + [2 * modes]
    halves = [slice(0, plane // 2), slice(plane // 2, plane)]

    def planes(slot, lanes):
        return [fields[slot, i * GROUP : (i + 1) * GROUP, lanes] for i in range(VSIDE)]

    for start in range(0, nodes, GROUP):
        group = slice(start, start + GROUP)
        values = dist_ref[:, group, :].reshape(VSIDE * GROUP, plane)
        fields[0] = dot(values, into_ref[0]) + dot(values, into_ref[1])
        for lanes in halves:
            for i, part in enumerate(cosine_forward(planes(0, lanes))):
                spectrum[i, :, lanes] = part

        def filtered(which, slot):
            parts = [
                (spectrum[i] * kern_ref[which, i : i + 1, :]).astype(jnp.bfloat16)
                for i in range(VSIDE)
            ]
            left = jnp.concatenate(parts, axis=0)
            fields[slot] = dot(left, back_ref[0]) + dot(left, back_ref[1])

        def gathered(which, slot):
            for lanes in halves:
                for i, field in enumerate(cosine_backward(planes(slot, lanes))):
                    if which < modes:
                        first[i, :, lanes] = field
                    elif which == modes:
                        gain[i, :, lanes] = first[i, :, lanes] * field
                    elif which < 2 * modes:
                        gain[i, :, lanes] = gain[i, :, lanes] + first[i, :, lanes] * field
                    else:
                        value = dist_ref[i, group, lanes].astype(jnp.float32)
                        total = value + relax_step * (gain[i, :, lanes] - value * field)
                        out_ref[i, group, lanes] = total.astype(jnp.bfloat16)

        filtered(order[0], 0)
        for at, which in enumerate(order):
            if at + 1 < len(order):
                filtered(order[at + 1], (at + 1) % 2)
            gathered(which, at % 2)


def in_vmem():
    return pl.BlockSpec(memory_space=pltpu.VMEM)


def in_smem():
    return pl.BlockSpec(memory_space=pltpu.SMEM)


def on_chip(array):
    return pltpu.with_memory_space_constraint(array, pltpu.VMEM)


def on_device(dist, send_faces, send_count, source_face, subface, alpha, beta):
    elements, nodes, width = dist.shape
    faces = 6 * elements
    gradients, _, _ = static_tables()
    traces = pltpu.VMEM((SLOTS, 16, width), jnp.bfloat16)

    back, ahead, held, rows = pl.pallas_call(
        send_kernel,
        out_shape=(
            traces,
            traces,
            pltpu.VMEM(dist.shape, jnp.bfloat16),
            pltpu.VMEM((faces, 16, width), jnp.bfloat16),
        ),
        in_specs=[in_smem(), in_smem(), pl.BlockSpec(memory_space=pl.ANY)],
        out_specs=(in_vmem(),) * 4,
        scratch_shapes=[pltpu.SemaphoreType.DMA((PIECES,))],
        name="send_traces",
    )(send_faces, send_count, dist)
    from_prev = passed_along(ahead, "space", 1)
    from_next = passed_along(back, "space", -1)

    sources, levels = source_face.T, subface.T
    lifts = on_chip(jnp.asarray(mortar_lifts()))
    gradient = on_chip(jnp.asarray(gradients.reshape(3 * nodes, nodes), jnp.bfloat16))
    part = pl.pallas_call(
        local_kernel,
        out_shape=pltpu.VMEM(dist.shape, jnp.float32),
        in_specs=[in_smem(), in_smem()] + [in_vmem()] * 4,
        out_specs=in_vmem(),
        scratch_shapes=[
            pltpu.VMEM((faces + 1, 16, width), jnp.bfloat16),
            pltpu.VMEM((elements, 128, width), jnp.bfloat16),
        ],
        name="transport_local",
    )(sources, levels, on_chip(held), on_chip(rows), gradient, lifts)
    updated = pl.pallas_call(
        remote_kernel,
        out_shape=pltpu.VMEM(dist.shape, jnp.bfloat16),
        in_specs=[in_smem(), in_smem()] + [in_vmem()] * 4,
        out_specs=in_vmem(),
        scratch_shapes=[
            pltpu.VMEM((2 * SLOTS + 1, 16, width), jnp.bfloat16),
            pltpu.VMEM((elements, 128, width), jnp.bfloat16),
        ],
        name="transport_remote",
    )(sources, levels, on_chip(part), on_chip(from_prev), on_chip(from_next), lifts)

    plane = VSIDE * VSIDE
    cosine = cosine_table()
    pair = np.kron(cosine, cosine)
    into = on_chip(jnp.asarray(np.stack(split_table(pair.T))))
    out_of = on_chip(jnp.asarray(np.stack(split_table(pair))))
    norms = np.full((VSIDE, 1), 2.0 / VSIDE, np.float32)
    norms[0] = 1.0 / VSIDE
    kernels = jnp.concatenate([alpha, beta], axis=0).reshape(-1, VSIDE, plane) * norms
    whole = lax.all_to_all(updated, "vel", split_axis=0, concat_axis=0, tiled=True)
    cube = pltpu.VMEM((VSIDE, GROUP, plane), jnp.float32)
    mixed = pl.pallas_call(
        collide_kernel,
        out_shape=pltpu.VMEM(whole.shape, jnp.bfloat16),
        in_specs=[in_vmem()] * 4,
        out_specs=in_vmem(),
        scratch_shapes=[cube, pltpu.VMEM((2, VSIDE * GROUP, plane), jnp.float32), cube, cube],
        name="collide",
    )(on_chip(whole), on_chip(kernels), into, out_of)
    return lax.all_to_all(mixed, "vel", split_axis=0, concat_axis=0, tiled=True)


def solution(mesh):
    return jax.shard_map(
        on_device,
        mesh=mesh,
        in_specs=(
            P("space", None, "vel"),
            P("space", None, None),
            P("space", None),
            P("space", None),
            P("space", None),
            P(),
            P(),
        ),
        out_specs=P("space", None, "vel"),
        check_vma=False,
    )
```

```python
import jax
import jax.numpy as jnp
import ml_dtypes
import numpy as np
from jax import lax
from jax.experimental import pallas as pl
from jax.experimental.pallas import tpu as pltpu
from jax.sharding import PartitionSpec as P

VSIDE = 16
SLOTS = 16
GROUP = 16
SCOPED = 16 << 20


courant = 0.1
lift_weight = 6.0
relax_step = 0.5


def passed_along(block, axis, distance):
    devices = range(lax.axis_size(axis))
    route = [((i - distance) % len(devices), i) for i in devices]
    return lax.ppermute(block, axis, route)


def lobatto_points():
    return np.array([-1.0, -1.0 / np.sqrt(5.0), 1.0 / np.sqrt(5.0), 1.0])


def lagrange_table(targets):
    points = lobatto_points()
    result = np.ones((targets.shape[0], 4))
    for column in range(4):
        for second in range(4):
            if second != column:
                result[:, column] = (
                    result[:, column]
                    * (targets - points[second])
                    / (points[column] - points[second])
                )
    return result


def derivative_table():
    points = lobatto_points()
    result = np.zeros((4, 4))
    for row_at in range(4):
        for column in range(4):
            total = 0.0
            for skipped in range(4):
                if skipped != column:
                    factor = 1.0 / (points[column] - points[skipped])
                    for second in range(4):
                        if second != column and second != skipped:
                            factor = (
                                factor
                                * (points[row_at] - points[second])
                                / (points[column] - points[second])
                            )
                    total = total + factor
            result[row_at, column] = total
    return result


def cosine_table():
    index_list = np.arange(VSIDE)
    result = np.sqrt(2.0 / VSIDE) * np.cos(
        np.pi * (index_list[None, :] + 0.5) * index_list[:, None] / VSIDE
    )
    result[0] = result[0] / np.sqrt(2.0)
    return result


def static_tables():
    derivative = derivative_table()
    eye_four = np.eye(4)
    gradients = np.stack(
        [
            np.kron(np.kron(derivative, eye_four), eye_four),
            np.kron(np.kron(eye_four, derivative), eye_four),
            np.kron(np.kron(eye_four, eye_four), derivative),
        ]
    )
    selector = np.zeros((96, 64))
    for axis_at in range(3):
        for side_at in range(2):
            filled = 0
            for node_at in range(64):
                digits = (node_at // 16, node_at // 4 % 4, node_at % 4)
                if digits[axis_at] == 3 * side_at:
                    selector[(2 * axis_at + side_at) * 16 + filled, node_at] = 1.0
                    filled = filled + 1
    points = lobatto_points()
    halves = [lagrange_table((points - 1.0) / 2.0), lagrange_table((points + 1.0) / 2.0)]
    mortar = np.stack(
        [np.eye(16)]
        + [np.kron(halves[(which - 1) // 2], halves[(which - 1) % 2]) for which in range(1, 5)]
    )
    return (gradients, selector, mortar)


def split_table(table):
    high = np.asarray(table, np.float32).astype(ml_dtypes.bfloat16)
    rest = np.asarray(table, np.float64) - high.astype(np.float64)
    return (high, np.asarray(rest, np.float32).astype(ml_dtypes.bfloat16))


def mortar_lifts():
    _, selector, mortar = static_tables()
    tables = np.zeros((6, 5, 64, 128))
    for face in range(6):
        lift = selector[face * 16 : face * 16 + 16].T
        sign = -1.0 if face % 2 == 0 else 1.0
        for level in range(5):
            tables[face, level, :, face * 16 : face * 16 + 16] = sign * (lift @ mortar[level])
    return tables.astype(np.float32).astype(ml_dtypes.bfloat16)


def cosine_forward(values):
    count = len(values)
    if count == 1:
        return values
    half = count // 2
    sums = [values[i] + values[count - 1 - i] for i in range(half)]
    gaps = [
        (values[i] - values[count - 1 - i]) * float(0.5 / np.cos((i + 0.5) * np.pi / count))
        for i in range(half)
    ]
    even, odd = cosine_forward(sums), cosine_forward(gaps)
    result = []
    for i in range(half):
        result.append(even[i])
        result.append(odd[i] + odd[i + 1] if i + 1 < half else odd[i])
    return result


def cosine_backward(values):
    count = len(values)
    if count == 1:
        return values
    half = count // 2
    even = [values[2 * i] for i in range(half)]
    odd = [values[1]] + [values[2 * i - 1] + values[2 * i + 1] for i in range(1, half)]
    sums, gaps = cosine_backward(even), cosine_backward(odd)
    scaled = [gaps[i] * float(0.5 / np.cos((i + 0.5) * np.pi / count)) for i in range(half)]
    return [sums[i] + scaled[i] for i in range(half)] + [
        sums[half - 1 - i] - scaled[half - 1 - i] for i in range(half)
    ]


def dot(left, right):
    return jnp.dot(left, right, preferred_element_type=jnp.float32)


def face_nodes(face, shape, along):
    at = lax.broadcasted_iota(jnp.int32, shape, along)
    axis, side = face // 2, face % 2
    if axis == 0:
        return at + 48 * side
    high, low = at >> 2, at & 3
    return 16 * high + 12 * side + low if axis == 1 else 16 * high + 4 * low + 3 * side


def local_speeds(shape):
    index = lax.axis_index("vel") * shape[-1] + lax.broadcasted_iota(jnp.int32, shape, len(shape) - 1)
    along = [index // (VSIDE * VSIDE), (index // VSIDE) & (VSIDE - 1), index & (VSIDE - 1)]
    return [(entry.astype(jnp.float32) + 0.5) * (2.0 / VSIDE) - 1.0 for entry in along]


def inflow_faces(speeds):
    return [speeds[f // 2] > 0.0 if f % 2 == 0 else speeds[f // 2] < 0.0 for f in range(6)]


def inflow_masks(shape):
    ones = [jnp.where(on, 1.0, 0.0) for on in inflow_faces(local_speeds(shape))]
    return [one.astype(jnp.bfloat16) for one in ones]


def fetched(sems, *pairs):
    copies = [pltpu.make_async_copy(src, dst, sems.at[i]) for i, (src, dst) in enumerate(pairs)]
    for copy in copies:
        copy.start()
    return copies


def face_selector(nodes):
    node = lax.broadcasted_iota(jnp.int32, (16, nodes), 1)
    picks = [jnp.where(face_nodes(f, (16, nodes), 0) == node, 1.0, 0.0) for f in range(6)]
    return jnp.concatenate(picks, axis=0).astype(jnp.bfloat16)


def extract_traces(held, rows):
    elements, nodes, width = held.shape
    select = face_selector(nodes)
    for at in range(elements):
        traces = dot(select, held[at]).astype(jnp.bfloat16)
        rows[6 * at : 6 * at + 6] = traces.reshape(6, 16, width)


def send_kernel(faces_hbm, count_hbm, dist_hbm, back_ref, ahead_ref, held, rows, faces, count, sems):
    copies = fetched(sems, (faces_hbm, faces), (count_hbm, count), (dist_hbm, held))
    for copy in copies:
        copy.wait()
    extract_traces(held, rows)
    for way, out in enumerate((back_ref, ahead_ref)):
        for slot in range(SLOTS):
            keep = jnp.where(slot < count[0, way], 1.0, 0.0).astype(jnp.bfloat16)
            out[slot] = rows[faces[0, way, slot]] * keep


def add_lifts(left, stacked, total):
    speeds = local_speeds((1, total.shape[-1]))
    lifted = dot(left, stacked)
    for axis in range(3):
        weight = -courant * lift_weight * speeds[axis]
        total = total + lifted[64 * axis : 64 * axis + 64] * weight
    return total


def local_kernel(
    source_hbm,
    level_hbm,
    dist_hbm,
    gradient_ref,
    lift_ref,
    out_ref,
    left_ref,
    held,
    rows,
    stack,
    source,
    level,
    sems,
):
    copies = fetched(sems, (source_hbm, source), (level_hbm, level), (dist_hbm, held))
    elements, nodes, width = held.shape
    faces = 6 * elements
    speeds = local_speeds((1, width))
    masks = inflow_masks((16, width))
    wide = local_speeds((nodes, width))
    node = lax.broadcasted_iota(jnp.int32, (nodes, width), 0)
    digits = [node >> 4, (node >> 2) & 3, node & 3]
    loss = jnp.zeros((nodes, width), jnp.float32)
    for face, on in enumerate(inflow_faces(wide)):
        member = jnp.logical_and(on, digits[face // 2] == 3 * (face % 2))
        loss = loss + jnp.where(member, jnp.abs(wide[face // 2]), 0.0)
    keep = 1.0 - courant * lift_weight * loss
    for copy in copies:
        copy.wait()
    extract_traces(held, rows)
    rows[faces] = jnp.zeros((16, width), jnp.bfloat16)
    for at in range(elements):
        for face in range(6):
            trace = rows[jnp.minimum(source[face, at], faces)] * masks[face]
            stack[at, 16 * face : 16 * face + 16] = trace
        stack[at, 96:] = jnp.zeros((32, width), jnp.bfloat16)
        total = held[at].astype(jnp.float32) * keep
        moved = dot(gradient_ref[...], held[at])
        for axis in range(3):
            total = total + moved[64 * axis : 64 * axis + 64] * (-courant * speeds[axis])
        left = jnp.concatenate(
            [
                lift_ref[2 * axis, level[2 * axis, at]] + lift_ref[2 * axis + 1, level[2 * axis + 1, at]]
                for axis in range(3)
            ],
            axis=0,
        )
        left_ref[at] = left
        out_ref[at] = add_lifts(left, stack[at], total)


def remote_kernel(
    source_hbm, part_ref, left_ref, prev_ref, next_ref, out_ref, table, stack, source, sems
):
    copies = fetched(sems, (source_hbm, source))
    elements, _, width = part_ref.shape
    faces = 6 * elements
    table[0] = jnp.zeros((16, width), jnp.bfloat16)
    table[1 : SLOTS + 1] = prev_ref[...]
    table[SLOTS + 1 :] = next_ref[...]
    masks = inflow_masks((16, width))
    for copy in copies:
        copy.wait()
    for at in range(elements):
        for face in range(6):
            trace = table[jnp.maximum(source[face, at] - (faces - 1), 0)] * masks[face]
            stack[at, 16 * face : 16 * face + 16] = trace
        stack[at, 96:] = jnp.zeros((32, width), jnp.bfloat16)
        out_ref[at] = add_lifts(left_ref[at], stack[at], part_ref[at]).astype(jnp.bfloat16)


def collide_kernel(
    dist_ref, alpha_ref, beta_ref, into_ref, back_ref, out_ref, spectrum, fields, first, gain
):
    nodes, plane = dist_ref.shape[1], dist_ref.shape[2]
    modes = alpha_ref.shape[0]
    order = [m for pair in range(modes) for m in (pair, modes + pair)] + [2 * modes]
    halves = [slice(0, plane // 2), slice(plane // 2, plane)]

    def planes(slot, lanes):
        return [fields[slot, i * GROUP : (i + 1) * GROUP, lanes] for i in range(VSIDE)]

    for start in range(0, nodes, GROUP):
        group = slice(start, start + GROUP)
        values = dist_ref[:, group, :].reshape(VSIDE * GROUP, plane)
        fields[0] = dot(values, into_ref[0]) + dot(values, into_ref[1])
        for lanes in halves:
            for i, part in enumerate(cosine_forward(planes(0, lanes))):
                spectrum[i, :, lanes] = part if i else 0.5 * part

        def filtered(which, slot):
            kern = alpha_ref if which < modes else beta_ref
            row = which % modes if which < 2 * modes else modes
            parts = [
                (spectrum[i] * kern[row : row + 1, i * plane : (i + 1) * plane]).astype(jnp.bfloat16)
                for i in range(VSIDE)
            ]
            left = jnp.concatenate(parts, axis=0)
            fields[slot] = dot(left, back_ref[0]) + dot(left, back_ref[1])

        def gathered(which, slot):
            for lanes in halves:
                for i, field in enumerate(cosine_backward(planes(slot, lanes))):
                    if which < modes:
                        first[i, :, lanes] = field
                    elif which == modes:
                        gain[i, :, lanes] = first[i, :, lanes] * field
                    elif which < 2 * modes:
                        gain[i, :, lanes] = gain[i, :, lanes] + first[i, :, lanes] * field
                    else:
                        value = dist_ref[i, group, lanes].astype(jnp.float32)
                        total = value + relax_step * (gain[i, :, lanes] - value * field)
                        out_ref[i, group, lanes] = total.astype(jnp.bfloat16)

        filtered(order[0], 0)
        for at, which in enumerate(order):
            if at + 1 < len(order):
                filtered(order[at + 1], (at + 1) % 2)
            gathered(which, at % 2)


def in_vmem():
    return pl.BlockSpec(memory_space=pltpu.VMEM)


def in_hbm():
    return pl.BlockSpec(memory_space=pltpu.HBM)


def on_chip(array):
    return pltpu.with_memory_space_constraint(array, pltpu.VMEM)


def off_chip(*arrays):
    return [pltpu.with_memory_space_constraint(array, pltpu.HBM) for array in arrays]


def on_device(dist, send_faces, send_count, source_face, subface, alpha, beta):
    elements, nodes, width = dist.shape
    faces = 6 * elements
    gradients, _, _ = static_tables()
    traces = pltpu.VMEM((SLOTS, 16, width), jnp.bfloat16)
    block = pltpu.VMEM(dist.shape, jnp.bfloat16)

    back, ahead = pl.pallas_call(
        send_kernel,
        out_shape=(traces, traces),
        in_specs=[in_hbm()] * 3,
        out_specs=(in_vmem(), in_vmem()),
        scratch_shapes=[
            block,
            pltpu.VMEM((faces, 16, width), jnp.bfloat16),
            pltpu.SMEM(send_faces.shape, jnp.int32),
            pltpu.SMEM(send_count.shape, jnp.int32),
            pltpu.SemaphoreType.DMA((3,)),
        ],
        compiler_params=pltpu.CompilerParams(vmem_limit_bytes=SCOPED),
        name="send_traces",
    )(*off_chip(send_faces, send_count, dist))
    from_prev = passed_along(ahead, "space", 1)
    from_next = passed_along(back, "space", -1)

    sources, levels = source_face.T, subface.T
    lifts = jnp.asarray(mortar_lifts())
    gradient = jnp.asarray(gradients.reshape(3 * nodes, nodes), jnp.bfloat16)
    indices = pltpu.SMEM(sources.shape, jnp.int32)
    part, left = pl.pallas_call(
        local_kernel,
        out_shape=(
            pltpu.VMEM(dist.shape, jnp.float32),
            pltpu.VMEM((elements, 3 * nodes, 128), jnp.bfloat16),
        ),
        in_specs=[in_hbm()] * 3 + [in_vmem()] * 2,
        out_specs=(in_vmem(), in_vmem()),
        scratch_shapes=[
            block,
            pltpu.VMEM((faces + 1, 16, width), jnp.bfloat16),
            pltpu.VMEM((elements, 128, width), jnp.bfloat16),
            indices,
            indices,
            pltpu.SemaphoreType.DMA((3,)),
        ],
        compiler_params=pltpu.CompilerParams(vmem_limit_bytes=SCOPED),
        name="transport_local",
    )(*off_chip(sources, levels, dist), on_chip(gradient), on_chip(lifts))
    updated = pl.pallas_call(
        remote_kernel,
        out_shape=block,
        in_specs=[in_hbm()] + [in_vmem()] * 4,
        out_specs=in_vmem(),
        scratch_shapes=[
            pltpu.VMEM((2 * SLOTS + 1, 16, width), jnp.bfloat16),
            pltpu.VMEM((elements, 128, width), jnp.bfloat16),
            indices,
            pltpu.SemaphoreType.DMA((1,)),
        ],
        compiler_params=pltpu.CompilerParams(vmem_limit_bytes=SCOPED),
        name="transport_remote",
    )(*off_chip(sources), on_chip(part), on_chip(left), on_chip(from_prev), on_chip(from_next))

    plane = VSIDE * VSIDE
    cosine = cosine_table()
    pair = np.kron(cosine, cosine)
    into = jnp.asarray(np.stack(split_table(pair.T * (2.0 / VSIDE))))
    out_of = jnp.asarray(np.stack(split_table(pair)))
    whole = lax.all_to_all(updated, "vel", split_axis=0, concat_axis=0, tiled=True)
    cube = pltpu.VMEM((VSIDE, GROUP, plane), jnp.float32)
    mixed = pl.pallas_call(
        collide_kernel,
        out_shape=pltpu.VMEM(whole.shape, jnp.bfloat16),
        in_specs=[in_vmem()] * 5,
        out_specs=in_vmem(),
        scratch_shapes=[cube, pltpu.VMEM((2, VSIDE * GROUP, plane), jnp.float32), cube, cube],
        compiler_params=pltpu.CompilerParams(vmem_limit_bytes=SCOPED),
        name="collide",
    )(*[on_chip(array) for array in (whole, alpha, beta, into, out_of)])
    return lax.all_to_all(mixed, "vel", split_axis=0, concat_axis=0, tiled=True)


def solution(mesh):
    return jax.shard_map(
        on_device,
        mesh=mesh,
        in_specs=(
            P("space", None, "vel"),
            P("space", None, None),
            P("space", None),
            P("space", None),
            P("space", None),
            P(),
            P(),
        ),
        out_specs=P("space", None, "vel"),
        check_vma=False,
    )
```

```python
import jax
import jax.numpy as jnp
import ml_dtypes
import numpy as np
from jax import lax
from jax.experimental import pallas as pl
from jax.experimental.pallas import tpu as pltpu
from jax.sharding import PartitionSpec as P

VSIDE = 16
SLOTS = 16
GROUP = 16
SCOPED = 16 << 20


courant = 0.1
lift_weight = 6.0
relax_step = 0.5


def passed_along(block, axis, distance):
    devices = range(lax.axis_size(axis))
    route = [((i - distance) % len(devices), i) for i in devices]
    return lax.ppermute(block, axis, route)


def lobatto_points():
    return np.array([-1.0, -1.0 / np.sqrt(5.0), 1.0 / np.sqrt(5.0), 1.0])


def lagrange_table(targets):
    points = lobatto_points()
    result = np.ones((targets.shape[0], 4))
    for column in range(4):
        for second in range(4):
            if second != column:
                result[:, column] = (
                    result[:, column]
                    * (targets - points[second])
                    / (points[column] - points[second])
                )
    return result


def derivative_table():
    points = lobatto_points()
    result = np.zeros((4, 4))
    for row_at in range(4):
        for column in range(4):
            total = 0.0
            for skipped in range(4):
                if skipped != column:
                    factor = 1.0 / (points[column] - points[skipped])
                    for second in range(4):
                        if second != column and second != skipped:
                            factor = (
                                factor
                                * (points[row_at] - points[second])
                                / (points[column] - points[second])
                            )
                    total = total + factor
            result[row_at, column] = total
    return result


def cosine_table():
    index_list = np.arange(VSIDE)
    result = np.sqrt(2.0 / VSIDE) * np.cos(
        np.pi * (index_list[None, :] + 0.5) * index_list[:, None] / VSIDE
    )
    result[0] = result[0] / np.sqrt(2.0)
    return result


def static_tables():
    derivative = derivative_table()
    eye_four = np.eye(4)
    gradients = np.stack(
        [
            np.kron(np.kron(derivative, eye_four), eye_four),
            np.kron(np.kron(eye_four, derivative), eye_four),
            np.kron(np.kron(eye_four, eye_four), derivative),
        ]
    )
    selector = np.zeros((96, 64))
    for axis_at in range(3):
        for side_at in range(2):
            filled = 0
            for node_at in range(64):
                digits = (node_at // 16, node_at // 4 % 4, node_at % 4)
                if digits[axis_at] == 3 * side_at:
                    selector[(2 * axis_at + side_at) * 16 + filled, node_at] = 1.0
                    filled = filled + 1
    points = lobatto_points()
    halves = [lagrange_table((points - 1.0) / 2.0), lagrange_table((points + 1.0) / 2.0)]
    mortar = np.stack(
        [np.eye(16)]
        + [np.kron(halves[(which - 1) // 2], halves[(which - 1) % 2]) for which in range(1, 5)]
    )
    return (gradients, selector, mortar)


def split_table(table):
    high = np.asarray(table, np.float32).astype(ml_dtypes.bfloat16)
    rest = np.asarray(table, np.float64) - high.astype(np.float64)
    return (high, np.asarray(rest, np.float32).astype(ml_dtypes.bfloat16))


def transport_tables():
    gradients, selector, mortar = static_tables()
    tables = np.zeros((33, 64, 128))
    for face in range(6):
        lift = selector[face * 16 : face * 16 + 16].T
        sign = -1.0 if face % 2 == 0 else 1.0
        for level in range(5):
            placed = sign * (lift @ mortar[level])
            tables[5 * face + level, :, face * 16 : face * 16 + 16] = placed
    tables[30:, :, :64] = gradients
    return tables.astype(np.float32).astype(ml_dtypes.bfloat16)


def cosine_forward(values):
    count = len(values)
    if count == 1:
        return values
    half = count // 2
    sums = [values[i] + values[count - 1 - i] for i in range(half)]
    gaps = [
        (values[i] - values[count - 1 - i]) * float(0.5 / np.cos((i + 0.5) * np.pi / count))
        for i in range(half)
    ]
    even, odd = cosine_forward(sums), cosine_forward(gaps)
    result = []
    for i in range(half):
        result.append(even[i])
        result.append(odd[i] + odd[i + 1] if i + 1 < half else odd[i])
    return result


def cosine_backward(values):
    count = len(values)
    if count == 1:
        return values
    half = count // 2
    even = [values[2 * i] for i in range(half)]
    odd = [values[1]] + [values[2 * i - 1] + values[2 * i + 1] for i in range(1, half)]
    sums, gaps = cosine_backward(even), cosine_backward(odd)
    scaled = [gaps[i] * float(0.5 / np.cos((i + 0.5) * np.pi / count)) for i in range(half)]
    return [sums[i] + scaled[i] for i in range(half)] + [
        sums[half - 1 - i] - scaled[half - 1 - i] for i in range(half)
    ]


def dot(left, right):
    return jnp.dot(left, right, preferred_element_type=jnp.float32)


def face_nodes(face, shape, along):
    at = lax.broadcasted_iota(jnp.int32, shape, along)
    axis, side = face // 2, face % 2
    if axis == 0:
        return at + 48 * side
    high, low = at >> 2, at & 3
    return 16 * high + 12 * side + low if axis == 1 else 16 * high + 4 * low + 3 * side


def local_speeds(shape):
    index = lax.axis_index("vel") * shape[-1] + lax.broadcasted_iota(jnp.int32, shape, len(shape) - 1)
    along = [index // (VSIDE * VSIDE), (index // VSIDE) & (VSIDE - 1), index & (VSIDE - 1)]
    return [(entry.astype(jnp.float32) + 0.5) * (2.0 / VSIDE) - 1.0 for entry in along]


def inflow_faces(speeds):
    return [speeds[f // 2] > 0.0 if f % 2 == 0 else speeds[f // 2] < 0.0 for f in range(6)]


def inflow_masks(shape):
    ones = [jnp.where(on, 1.0, 0.0) for on in inflow_faces(local_speeds(shape))]
    return [one.astype(jnp.bfloat16) for one in ones]


def fetched(sems, *pairs):
    copies = [pltpu.make_async_copy(src, dst, sems.at[i]) for i, (src, dst) in enumerate(pairs)]
    for copy in copies:
        copy.start()
    return copies


def face_selector(nodes):
    node = lax.broadcasted_iota(jnp.int32, (16, nodes), 1)
    picks = [jnp.where(face_nodes(f, (16, nodes), 0) == node, 1.0, 0.0) for f in range(6)]
    return jnp.concatenate(picks, axis=0).astype(jnp.bfloat16)


def extract_traces(held, rows):
    elements, nodes, width = held.shape
    select = face_selector(nodes)
    for at in range(elements):
        traces = dot(select, held[at]).astype(jnp.bfloat16)
        rows[6 * at : 6 * at + 6] = traces.reshape(6, 16, width)


def send_kernel(faces_hbm, count_hbm, dist_hbm, back_ref, ahead_ref, held, rows, faces, count, sems):
    copies = fetched(sems, (faces_hbm, faces), (count_hbm, count), (dist_hbm, held))
    for copy in copies:
        copy.wait()
    extract_traces(held, rows)
    rows[6 * held.shape[0]] = jnp.zeros(rows.shape[1:], jnp.bfloat16)
    for way, out in enumerate((back_ref, ahead_ref)):
        for slot in range(SLOTS):
            keep = jnp.where(slot < count[0, way], 1.0, 0.0).astype(jnp.bfloat16)
            out[slot] = rows[faces[0, way, slot]] * keep


def add_lifts(left, stacked, total):
    speeds = local_speeds((1, total.shape[-1]))
    lifted = dot(left, stacked)
    for axis in range(3):
        weight = -courant * lift_weight * speeds[axis]
        total = total + lifted[64 * axis : 64 * axis + 64] * weight
    return total


def local_kernel(
    source_hbm, level_hbm, held, rows, table_ref, out_ref, left_ref, stack, source, level, sems
):
    copies = fetched(sems, (source_hbm, source), (level_hbm, level))
    elements, nodes, width = held.shape
    faces = 6 * elements
    speeds = local_speeds((1, width))
    masks = inflow_masks((16, width))
    wide = local_speeds((nodes, width))
    node = lax.broadcasted_iota(jnp.int32, (nodes, width), 0)
    digits = [node >> 4, (node >> 2) & 3, node & 3]
    loss = jnp.zeros((nodes, width), jnp.float32)
    for face, on in enumerate(inflow_faces(wide)):
        member = jnp.logical_and(on, digits[face // 2] == 3 * (face % 2))
        loss = loss + jnp.where(member, jnp.abs(wide[face // 2]), 0.0)
    keep = 1.0 - courant * lift_weight * loss
    for copy in copies:
        copy.wait()
    gradient = table_ref[30:].reshape(3 * nodes, table_ref.shape[2])[:, :nodes]
    for at in range(elements):
        for face in range(6):
            trace = rows[jnp.minimum(source[face, at], faces)] * masks[face]
            stack[at, 16 * face : 16 * face + 16] = trace
        stack[at, 96:] = jnp.zeros((32, width), jnp.bfloat16)
        total = held[at].astype(jnp.float32) * keep
        moved = dot(gradient, held[at])
        for axis in range(3):
            total = total + moved[64 * axis : 64 * axis + 64] * (-courant * speeds[axis])
        left = jnp.concatenate(
            [
                table_ref[10 * axis + level[2 * axis, at]]
                + table_ref[10 * axis + 5 + level[2 * axis + 1, at]]
                for axis in range(3)
            ],
            axis=0,
        )
        left_ref[at] = left
        out_ref[at] = add_lifts(left, stack[at], total)


def remote_kernel(
    source_hbm, part_ref, left_ref, prev_ref, next_ref, out_ref, table, stack, source, sems
):
    copies = fetched(sems, (source_hbm, source))
    elements, _, width = part_ref.shape
    faces = 6 * elements
    table[0] = jnp.zeros((16, width), jnp.bfloat16)
    table[1 : SLOTS + 1] = prev_ref[...]
    table[SLOTS + 1 :] = next_ref[...]
    masks = inflow_masks((16, width))
    for copy in copies:
        copy.wait()
    for at in range(elements):
        for face in range(6):
            trace = table[jnp.maximum(source[face, at] - (faces - 1), 0)] * masks[face]
            stack[at, 16 * face : 16 * face + 16] = trace
        stack[at, 96:] = jnp.zeros((32, width), jnp.bfloat16)
        out_ref[at] = add_lifts(left_ref[at], stack[at], part_ref[at]).astype(jnp.bfloat16)


def collide_kernel(
    dist_ref, alpha_ref, beta_ref, into_ref, back_ref, out_ref, spectrum, fields, first, gain
):
    nodes, plane = dist_ref.shape[1], dist_ref.shape[2]
    modes = alpha_ref.shape[0]
    order = [m for pair in range(modes) for m in (pair, modes + pair)] + [2 * modes]
    halves = [slice(0, plane // 2), slice(plane // 2, plane)]

    def planes(slot, lanes):
        return [fields[slot, i * GROUP : (i + 1) * GROUP, lanes] for i in range(VSIDE)]

    for start in range(0, nodes, GROUP):
        group = slice(start, start + GROUP)
        values = dist_ref[:, group, :].reshape(VSIDE * GROUP, plane)
        fields[0] = dot(values, into_ref[0]) + dot(values, into_ref[1])
        for lanes in halves:
            for i, part in enumerate(cosine_forward(planes(0, lanes))):
                spectrum[i, :, lanes] = part if i else 0.5 * part

        def filtered(which, slot):
            kern = alpha_ref if which < modes else beta_ref
            row = which % modes if which < 2 * modes else modes
            parts = [
                (spectrum[i] * kern[row : row + 1, i * plane : (i + 1) * plane]).astype(jnp.bfloat16)
                for i in range(VSIDE)
            ]
            left = jnp.concatenate(parts, axis=0)
            fields[slot] = dot(left, back_ref[0]) + dot(left, back_ref[1])

        def gathered(which, slot):
            for lanes in halves:
                for i, field in enumerate(cosine_backward(planes(slot, lanes))):
                    if which < modes:
                        first[i, :, lanes] = field
                    elif which == modes:
                        gain[i, :, lanes] = first[i, :, lanes] * field
                    elif which < 2 * modes:
                        gain[i, :, lanes] = gain[i, :, lanes] + first[i, :, lanes] * field
                    else:
                        value = dist_ref[i, group, lanes].astype(jnp.float32)
                        total = value + relax_step * (gain[i, :, lanes] - value * field)
                        out_ref[i, group, lanes] = total.astype(jnp.bfloat16)

        filtered(order[0], 0)
        for at, which in enumerate(order):
            if at + 1 < len(order):
                filtered(order[at + 1], (at + 1) % 2)
            gathered(which, at % 2)


def in_vmem():
    return pl.BlockSpec(memory_space=pltpu.VMEM)


def in_hbm():
    return pl.BlockSpec(memory_space=pltpu.HBM)


def on_chip(array):
    return pltpu.with_memory_space_constraint(array, pltpu.VMEM)


def off_chip(*arrays):
    return [pltpu.with_memory_space_constraint(array, pltpu.HBM) for array in arrays]


def on_device(dist, send_faces, send_count, source_face, subface, alpha, beta):
    elements, nodes, width = dist.shape
    faces = 6 * elements
    traces = pltpu.VMEM((SLOTS, 16, width), jnp.bfloat16)
    block = pltpu.VMEM(dist.shape, jnp.bfloat16)

    back, ahead, held, rows = pl.pallas_call(
        send_kernel,
        out_shape=(traces, traces, block, pltpu.VMEM((faces + 1, 16, width), jnp.bfloat16)),
        in_specs=[in_hbm()] * 3,
        out_specs=(in_vmem(),) * 4,
        scratch_shapes=[
            pltpu.SMEM(send_faces.shape, jnp.int32),
            pltpu.SMEM(send_count.shape, jnp.int32),
            pltpu.SemaphoreType.DMA((3,)),
        ],
        compiler_params=pltpu.CompilerParams(vmem_limit_bytes=SCOPED),
        name="send_traces",
    )(*off_chip(send_faces, send_count, dist))
    from_prev = passed_along(ahead, "space", 1)
    from_next = passed_along(back, "space", -1)

    sources, levels = source_face.T, subface.T
    indices = pltpu.SMEM(sources.shape, jnp.int32)
    part, left = pl.pallas_call(
        local_kernel,
        out_shape=(
            pltpu.VMEM(dist.shape, jnp.float32),
            pltpu.VMEM((elements, 3 * nodes, 128), jnp.bfloat16),
        ),
        in_specs=[in_hbm()] * 2 + [in_vmem()] * 3,
        out_specs=(in_vmem(), in_vmem()),
        scratch_shapes=[
            pltpu.VMEM((elements, 128, width), jnp.bfloat16),
            indices,
            indices,
            pltpu.SemaphoreType.DMA((2,)),
        ],
        compiler_params=pltpu.CompilerParams(vmem_limit_bytes=SCOPED),
        name="transport_local",
    )(*off_chip(sources, levels), on_chip(held), on_chip(rows), on_chip(jnp.asarray(transport_tables())))
    updated = pl.pallas_call(
        remote_kernel,
        out_shape=block,
        in_specs=[in_hbm()] + [in_vmem()] * 4,
        out_specs=in_vmem(),
        scratch_shapes=[
            pltpu.VMEM((2 * SLOTS + 1, 16, width), jnp.bfloat16),
            pltpu.VMEM((elements, 128, width), jnp.bfloat16),
            indices,
            pltpu.SemaphoreType.DMA((1,)),
        ],
        compiler_params=pltpu.CompilerParams(vmem_limit_bytes=SCOPED),
        name="transport_remote",
    )(*off_chip(sources), on_chip(part), on_chip(left), on_chip(from_prev), on_chip(from_next))

    plane = VSIDE * VSIDE
    cosine = cosine_table()
    pair = np.kron(cosine, cosine)
    into = jnp.asarray(np.stack(split_table(pair.T * (2.0 / VSIDE))))
    out_of = jnp.asarray(np.stack(split_table(pair)))
    whole = lax.all_to_all(updated, "vel", split_axis=0, concat_axis=0, tiled=True)
    cube = pltpu.VMEM((VSIDE, GROUP, plane), jnp.float32)
    mixed = pl.pallas_call(
        collide_kernel,
        out_shape=pltpu.VMEM(whole.shape, jnp.bfloat16),
        in_specs=[in_vmem()] * 5,
        out_specs=in_vmem(),
        scratch_shapes=[cube, pltpu.VMEM((2, VSIDE * GROUP, plane), jnp.float32), cube, cube],
        compiler_params=pltpu.CompilerParams(vmem_limit_bytes=SCOPED),
        name="collide",
    )(*[on_chip(array) for array in (whole, alpha, beta, into, out_of)])
    return lax.all_to_all(mixed, "vel", split_axis=0, concat_axis=0, tiled=True)


def solution(mesh):
    return jax.shard_map(
        on_device,
        mesh=mesh,
        in_specs=(
            P("space", None, "vel"),
            P("space", None, None),
            P("space", None),
            P("space", None),
            P("space", None),
            P(),
            P(),
        ),
        out_specs=P("space", None, "vel"),
        check_vma=False,
    )
```

```python
import jax
import jax.numpy as jnp
import ml_dtypes
import numpy as np
from jax import lax
from jax.experimental import pallas as pl
from jax.experimental.pallas import tpu as pltpu
from jax.sharding import PartitionSpec as P

VSIDE = 16
SLOTS = 16
GROUP = 16
SCOPED = 16 << 20


courant = 0.1
lift_weight = 6.0
relax_step = 0.5


def passed_along(block, axis, distance):
    devices = range(lax.axis_size(axis))
    route = [((i - distance) % len(devices), i) for i in devices]
    return lax.ppermute(block, axis, route)


def lobatto_points():
    return np.array([-1.0, -1.0 / np.sqrt(5.0), 1.0 / np.sqrt(5.0), 1.0])


def lagrange_table(targets):
    points = lobatto_points()
    result = np.ones((targets.shape[0], 4))
    for column in range(4):
        for second in range(4):
            if second != column:
                result[:, column] = (
                    result[:, column]
                    * (targets - points[second])
                    / (points[column] - points[second])
                )
    return result


def derivative_table():
    points = lobatto_points()
    result = np.zeros((4, 4))
    for row_at in range(4):
        for column in range(4):
            total = 0.0
            for skipped in range(4):
                if skipped != column:
                    factor = 1.0 / (points[column] - points[skipped])
                    for second in range(4):
                        if second != column and second != skipped:
                            factor = (
                                factor
                                * (points[row_at] - points[second])
                                / (points[column] - points[second])
                            )
                    total = total + factor
            result[row_at, column] = total
    return result


def cosine_table():
    index_list = np.arange(VSIDE)
    result = np.sqrt(2.0 / VSIDE) * np.cos(
        np.pi * (index_list[None, :] + 0.5) * index_list[:, None] / VSIDE
    )
    result[0] = result[0] / np.sqrt(2.0)
    return result


def static_tables():
    derivative = derivative_table()
    eye_four = np.eye(4)
    gradients = np.stack(
        [
            np.kron(np.kron(derivative, eye_four), eye_four),
            np.kron(np.kron(eye_four, derivative), eye_four),
            np.kron(np.kron(eye_four, eye_four), derivative),
        ]
    )
    selector = np.zeros((96, 64))
    for axis_at in range(3):
        for side_at in range(2):
            filled = 0
            for node_at in range(64):
                digits = (node_at // 16, node_at // 4 % 4, node_at % 4)
                if digits[axis_at] == 3 * side_at:
                    selector[(2 * axis_at + side_at) * 16 + filled, node_at] = 1.0
                    filled = filled + 1
    points = lobatto_points()
    halves = [lagrange_table((points - 1.0) / 2.0), lagrange_table((points + 1.0) / 2.0)]
    mortar = np.stack(
        [np.eye(16)]
        + [np.kron(halves[(which - 1) // 2], halves[(which - 1) % 2]) for which in range(1, 5)]
    )
    return (gradients, selector, mortar)


def split_table(table):
    high = np.asarray(table, np.float32).astype(ml_dtypes.bfloat16)
    rest = np.asarray(table, np.float64) - high.astype(np.float64)
    return (high, np.asarray(rest, np.float32).astype(ml_dtypes.bfloat16))


def transport_tables():
    gradients, selector, mortar = static_tables()
    tables = np.zeros((33, 64, 128))
    for face in range(6):
        lift = selector[face * 16 : face * 16 + 16].T
        sign = -1.0 if face % 2 == 0 else 1.0
        for level in range(5):
            placed = sign * (lift @ mortar[level])
            tables[5 * face + level, :, face * 16 : face * 16 + 16] = placed
    tables[30:, :, :64] = gradients
    return tables.astype(np.float32).astype(ml_dtypes.bfloat16)


def cosine_forward(values):
    count = len(values)
    if count == 1:
        return values
    half = count // 2
    sums = [values[i] + values[count - 1 - i] for i in range(half)]
    gaps = [
        (values[i] - values[count - 1 - i]) * float(0.5 / np.cos((i + 0.5) * np.pi / count))
        for i in range(half)
    ]
    even, odd = cosine_forward(sums), cosine_forward(gaps)
    result = []
    for i in range(half):
        result.append(even[i])
        result.append(odd[i] + odd[i + 1] if i + 1 < half else odd[i])
    return result


def cosine_backward(values):
    count = len(values)
    if count == 1:
        return values
    half = count // 2
    even = [values[2 * i] for i in range(half)]
    odd = [values[1]] + [values[2 * i - 1] + values[2 * i + 1] for i in range(1, half)]
    sums, gaps = cosine_backward(even), cosine_backward(odd)
    scaled = [gaps[i] * float(0.5 / np.cos((i + 0.5) * np.pi / count)) for i in range(half)]
    return [sums[i] + scaled[i] for i in range(half)] + [
        sums[half - 1 - i] - scaled[half - 1 - i] for i in range(half)
    ]


def dot(left, right):
    return jnp.dot(left, right, preferred_element_type=jnp.float32)


def face_nodes(face, shape, along):
    at = lax.broadcasted_iota(jnp.int32, shape, along)
    axis, side = face // 2, face % 2
    if axis == 0:
        return at + 48 * side
    high, low = at >> 2, at & 3
    return 16 * high + 12 * side + low if axis == 1 else 16 * high + 4 * low + 3 * side


def local_speeds(shape):
    index = lax.axis_index("vel") * shape[-1] + lax.broadcasted_iota(jnp.int32, shape, len(shape) - 1)
    along = [index // (VSIDE * VSIDE), (index // VSIDE) & (VSIDE - 1), index & (VSIDE - 1)]
    return [(entry.astype(jnp.float32) + 0.5) * (2.0 / VSIDE) - 1.0 for entry in along]


def inflow_faces(speeds):
    return [speeds[f // 2] > 0.0 if f % 2 == 0 else speeds[f // 2] < 0.0 for f in range(6)]


def inflow_masks(shape):
    ones = [jnp.where(on, 1.0, 0.0) for on in inflow_faces(local_speeds(shape))]
    return [one.astype(jnp.bfloat16) for one in ones]


def fetched(sems, *pairs):
    copies = [pltpu.make_async_copy(src, dst, sems.at[i]) for i, (src, dst) in enumerate(pairs)]
    for copy in copies:
        copy.start()
    return copies


def face_selector(nodes):
    node = lax.broadcasted_iota(jnp.int32, (16, nodes), 1)
    picks = [jnp.where(face_nodes(f, (16, nodes), 0) == node, 1.0, 0.0) for f in range(6)]
    return jnp.concatenate(picks, axis=0).astype(jnp.bfloat16)


def extract_traces(held, rows):
    elements, nodes, width = held.shape
    select = face_selector(nodes)
    for at in range(elements):
        traces = dot(select, held[at]).astype(jnp.bfloat16)
        rows[6 * at : 6 * at + 6] = traces.reshape(6, 16, width)


def send_kernel(
    faces_hbm,
    count_hbm,
    source_hbm,
    level_hbm,
    dist_hbm,
    back_ref,
    ahead_ref,
    held,
    rows,
    source,
    level,
    faces,
    count,
    sems,
):
    pairs = (faces_hbm, faces), (count_hbm, count), (dist_hbm, held), (source_hbm, source)
    copies = fetched(sems, *pairs, (level_hbm, level))
    for copy in copies:
        copy.wait()
    extract_traces(held, rows)
    rows[6 * held.shape[0]] = jnp.zeros(rows.shape[1:], jnp.bfloat16)
    for way, out in enumerate((back_ref, ahead_ref)):
        for slot in range(SLOTS):
            keep = jnp.where(slot < count[0, way], 1.0, 0.0).astype(jnp.bfloat16)
            out[slot] = rows[faces[0, way, slot]] * keep


def add_lifts(left, stacked, total):
    speeds = local_speeds((1, total.shape[-1]))
    lifted = dot(left, stacked)
    for axis in range(3):
        weight = -courant * lift_weight * speeds[axis]
        total = total + lifted[64 * axis : 64 * axis + 64] * weight
    return total


def local_kernel(source, level, held, rows, table_ref, out_ref, left_ref, stack):
    elements, nodes, width = held.shape
    faces = 6 * elements
    speeds = local_speeds((1, width))
    masks = inflow_masks((16, width))
    wide = local_speeds((nodes, width))
    node = lax.broadcasted_iota(jnp.int32, (nodes, width), 0)
    digits = [node >> 4, (node >> 2) & 3, node & 3]
    loss = jnp.zeros((nodes, width), jnp.float32)
    for face, on in enumerate(inflow_faces(wide)):
        member = jnp.logical_and(on, digits[face // 2] == 3 * (face % 2))
        loss = loss + jnp.where(member, jnp.abs(wide[face // 2]), 0.0)
    keep = 1.0 - courant * lift_weight * loss
    gradient = table_ref[30:].reshape(3 * nodes, table_ref.shape[2])[:, :nodes]
    for at in range(elements):
        for face in range(6):
            trace = rows[jnp.minimum(source[face, at], faces)] * masks[face]
            stack[at, 16 * face : 16 * face + 16] = trace
        stack[at, 96:] = jnp.zeros((32, width), jnp.bfloat16)
        total = held[at].astype(jnp.float32) * keep
        moved = dot(gradient, held[at])
        for axis in range(3):
            total = total + moved[64 * axis : 64 * axis + 64] * (-courant * speeds[axis])
        left = jnp.concatenate(
            [
                table_ref[10 * axis + level[2 * axis, at]]
                + table_ref[10 * axis + 5 + level[2 * axis + 1, at]]
                for axis in range(3)
            ],
            axis=0,
        )
        left_ref[at] = left
        out_ref[at] = add_lifts(left, stack[at], total)


def remote_kernel(source, part_ref, left_ref, prev_ref, next_ref, out_ref, table, stack):
    elements, _, width = part_ref.shape
    faces = 6 * elements
    table[0] = jnp.zeros((16, width), jnp.bfloat16)
    table[1 : SLOTS + 1] = prev_ref[...]
    table[SLOTS + 1 :] = next_ref[...]
    masks = inflow_masks((16, width))
    for at in range(elements):
        for face in range(6):
            trace = table[jnp.maximum(source[face, at] - (faces - 1), 0)] * masks[face]
            stack[at, 16 * face : 16 * face + 16] = trace
        stack[at, 96:] = jnp.zeros((32, width), jnp.bfloat16)
        out_ref[at] = add_lifts(left_ref[at], stack[at], part_ref[at]).astype(jnp.bfloat16)


def collide_kernel(dist_ref, alpha_ref, beta_ref, into_ref, back_ref, out_ref):
    nodes, plane = dist_ref.shape[1], dist_ref.shape[2]
    modes = alpha_ref.shape[0]

    def planes(array):
        cube = array.reshape(VSIDE, GROUP, plane)
        return [cube[i] for i in range(VSIDE)]

    for start in range(0, nodes, GROUP):
        group = slice(start, start + GROUP)
        values = dist_ref[:, group, :].reshape(VSIDE * GROUP, plane)
        spectrum = cosine_forward(planes(dot(values, into_ref[0]) + dot(values, into_ref[1])))
        spectrum[0] = 0.5 * spectrum[0]

        def field(kern, row):
            parts = [
                (spectrum[i] * kern[row : row + 1, i * plane : (i + 1) * plane]).astype(jnp.bfloat16)
                for i in range(VSIDE)
            ]
            left = jnp.concatenate(parts, axis=0)
            return cosine_backward(planes(dot(left, back_ref[0]) + dot(left, back_ref[1])))

        gain = None
        for mode in range(modes):
            pairs = zip(field(alpha_ref, mode), field(beta_ref, mode))
            products = [first * second for first, second in pairs]
            gain = products if mode == 0 else [a + b for a, b in zip(gain, products)]
        loss = field(beta_ref, modes)
        for i in range(VSIDE):
            value = dist_ref[i, group, :].astype(jnp.float32)
            total = value + relax_step * (gain[i] - value * loss[i])
            out_ref[i, group, :] = total.astype(jnp.bfloat16)


def in_vmem():
    return pl.BlockSpec(memory_space=pltpu.VMEM)


def in_hbm():
    return pl.BlockSpec(memory_space=pltpu.HBM)


def in_smem():
    return pl.BlockSpec(memory_space=pltpu.SMEM)


def on_chip(*arrays):
    return [pltpu.with_memory_space_constraint(array, pltpu.VMEM) for array in arrays]


def in_scalar(*arrays):
    return [pltpu.with_memory_space_constraint(array, pltpu.SMEM) for array in arrays]


def off_chip(*arrays):
    return [pltpu.with_memory_space_constraint(array, pltpu.HBM) for array in arrays]


def on_device(dist, send_faces, send_count, source_face, subface, alpha, beta):
    elements, nodes, width = dist.shape
    faces = 6 * elements
    traces = pltpu.VMEM((SLOTS, 16, width), jnp.bfloat16)
    block = pltpu.VMEM(dist.shape, jnp.bfloat16)

    sources, levels = source_face.T, subface.T
    indices = pltpu.SMEM(sources.shape, jnp.int32)
    back, ahead, held, rows, source, level = pl.pallas_call(
        send_kernel,
        out_shape=(
            traces,
            traces,
            block,
            pltpu.VMEM((faces + 1, 16, width), jnp.bfloat16),
            indices,
            indices,
        ),
        in_specs=[in_hbm()] * 5,
        out_specs=(in_vmem(),) * 4 + (in_smem(),) * 2,
        scratch_shapes=[
            pltpu.SMEM(send_faces.shape, jnp.int32),
            pltpu.SMEM(send_count.shape, jnp.int32),
            pltpu.SemaphoreType.DMA((5,)),
        ],
        compiler_params=pltpu.CompilerParams(vmem_limit_bytes=SCOPED),
        name="send_traces",
    )(*off_chip(send_faces, send_count, sources, levels, dist))
    from_prev = passed_along(ahead, "space", 1)
    from_next = passed_along(back, "space", -1)

    source, level = in_scalar(source, level)
    part, left = pl.pallas_call(
        local_kernel,
        out_shape=(
            pltpu.VMEM(dist.shape, jnp.float32),
            pltpu.VMEM((elements, 3 * nodes, 128), jnp.bfloat16),
        ),
        in_specs=[in_smem()] * 2 + [in_vmem()] * 3,
        out_specs=(in_vmem(), in_vmem()),
        scratch_shapes=[pltpu.VMEM((elements, 128, width), jnp.bfloat16)],
        compiler_params=pltpu.CompilerParams(vmem_limit_bytes=SCOPED),
        name="transport_local",
    )(source, level, *on_chip(held, rows, jnp.asarray(transport_tables())))
    updated = pl.pallas_call(
        remote_kernel,
        out_shape=block,
        in_specs=[in_smem()] + [in_vmem()] * 4,
        out_specs=in_vmem(),
        scratch_shapes=[
            pltpu.VMEM((2 * SLOTS + 1, 16, width), jnp.bfloat16),
            pltpu.VMEM((elements, 128, width), jnp.bfloat16),
        ],
        compiler_params=pltpu.CompilerParams(vmem_limit_bytes=SCOPED),
        name="transport_remote",
    )(source, *on_chip(part, left, from_prev, from_next))

    plane = VSIDE * VSIDE
    cosine = cosine_table()
    pair = np.kron(cosine, cosine)
    into = jnp.asarray(np.stack(split_table(pair.T * (2.0 / VSIDE))))
    out_of = jnp.asarray(np.stack(split_table(pair)))
    whole = lax.all_to_all(updated, "vel", split_axis=0, concat_axis=0, tiled=True)
    mixed = pl.pallas_call(
        collide_kernel,
        out_shape=pltpu.VMEM(whole.shape, jnp.bfloat16),
        in_specs=[in_vmem()] * 5,
        out_specs=in_vmem(),
        compiler_params=pltpu.CompilerParams(vmem_limit_bytes=SCOPED),
        name="collide",
    )(*on_chip(whole, alpha, beta, into, out_of))
    return lax.all_to_all(mixed, "vel", split_axis=0, concat_axis=0, tiled=True)


def solution(mesh):
    return jax.shard_map(
        on_device,
        mesh=mesh,
        in_specs=(
            P("space", None, "vel"),
            P("space", None, None),
            P("space", None),
            P("space", None),
            P("space", None),
            P(),
            P(),
        ),
        out_specs=P("space", None, "vel"),
        check_vma=False,
    )
```

```python
import jax
import jax.numpy as jnp
import ml_dtypes
import numpy as np
from jax import lax
from jax.experimental import pallas as pl
from jax.experimental.pallas import tpu as pltpu
from jax.sharding import PartitionSpec as P

VSIDE = 16
SLOTS = 16
GROUP = 16
SCOPED = 16 << 20


courant = 0.1
lift_weight = 6.0
relax_step = 0.5


def lobatto_points():
    return np.array([-1.0, -1.0 / np.sqrt(5.0), 1.0 / np.sqrt(5.0), 1.0])


def lagrange_table(targets):
    points = lobatto_points()
    result = np.ones((targets.shape[0], 4))
    for column in range(4):
        for second in range(4):
            if second != column:
                result[:, column] = (
                    result[:, column]
                    * (targets - points[second])
                    / (points[column] - points[second])
                )
    return result


def derivative_table():
    points = lobatto_points()
    result = np.zeros((4, 4))
    for row_at in range(4):
        for column in range(4):
            total = 0.0
            for skipped in range(4):
                if skipped != column:
                    factor = 1.0 / (points[column] - points[skipped])
                    for second in range(4):
                        if second != column and second != skipped:
                            factor = (
                                factor
                                * (points[row_at] - points[second])
                                / (points[column] - points[second])
                            )
                    total = total + factor
            result[row_at, column] = total
    return result


def cosine_table():
    index_list = np.arange(VSIDE)
    result = np.sqrt(2.0 / VSIDE) * np.cos(
        np.pi * (index_list[None, :] + 0.5) * index_list[:, None] / VSIDE
    )
    result[0] = result[0] / np.sqrt(2.0)
    return result


def static_tables():
    derivative = derivative_table()
    eye_four = np.eye(4)
    gradients = np.stack(
        [
            np.kron(np.kron(derivative, eye_four), eye_four),
            np.kron(np.kron(eye_four, derivative), eye_four),
            np.kron(np.kron(eye_four, eye_four), derivative),
        ]
    )
    selector = np.zeros((96, 64))
    for axis_at in range(3):
        for side_at in range(2):
            filled = 0
            for node_at in range(64):
                digits = (node_at // 16, node_at // 4 % 4, node_at % 4)
                if digits[axis_at] == 3 * side_at:
                    selector[(2 * axis_at + side_at) * 16 + filled, node_at] = 1.0
                    filled = filled + 1
    points = lobatto_points()
    halves = [lagrange_table((points - 1.0) / 2.0), lagrange_table((points + 1.0) / 2.0)]
    mortar = np.stack(
        [np.eye(16)]
        + [np.kron(halves[(which - 1) // 2], halves[(which - 1) % 2]) for which in range(1, 5)]
    )
    return (gradients, selector, mortar)


def split_table(table):
    high = np.asarray(table, np.float32).astype(ml_dtypes.bfloat16)
    rest = np.asarray(table, np.float64) - high.astype(np.float64)
    return (high, np.asarray(rest, np.float32).astype(ml_dtypes.bfloat16))


def transport_tables():
    gradients, selector, mortar = static_tables()
    tables = np.zeros((33, 64, 128))
    for face in range(6):
        lift = selector[face * 16 : face * 16 + 16].T
        sign = -1.0 if face % 2 == 0 else 1.0
        for level in range(5):
            placed = sign * (lift @ mortar[level])
            tables[5 * face + level, :, face * 16 : face * 16 + 16] = placed
    tables[30:, :, :64] = gradients
    return tables.astype(np.float32).astype(ml_dtypes.bfloat16)


def cosine_forward(values):
    count = len(values)
    if count == 1:
        return values
    half = count // 2
    sums = [values[i] + values[count - 1 - i] for i in range(half)]
    gaps = [
        (values[i] - values[count - 1 - i]) * float(0.5 / np.cos((i + 0.5) * np.pi / count))
        for i in range(half)
    ]
    even, odd = cosine_forward(sums), cosine_forward(gaps)
    result = []
    for i in range(half):
        result.append(even[i])
        result.append(odd[i] + odd[i + 1] if i + 1 < half else odd[i])
    return result


def cosine_backward(values):
    count = len(values)
    if count == 1:
        return values
    half = count // 2
    even = [values[2 * i] for i in range(half)]
    odd = [values[1]] + [values[2 * i - 1] + values[2 * i + 1] for i in range(1, half)]
    sums, gaps = cosine_backward(even), cosine_backward(odd)
    scaled = [gaps[i] * float(0.5 / np.cos((i + 0.5) * np.pi / count)) for i in range(half)]
    return [sums[i] + scaled[i] for i in range(half)] + [
        sums[half - 1 - i] - scaled[half - 1 - i] for i in range(half)
    ]


def dot(left, right):
    return jnp.dot(left, right, preferred_element_type=jnp.float32)


def face_nodes(face, shape, along):
    at = lax.broadcasted_iota(jnp.int32, shape, along)
    axis, side = face // 2, face % 2
    if axis == 0:
        return at + 48 * side
    high, low = at >> 2, at & 3
    return 16 * high + 12 * side + low if axis == 1 else 16 * high + 4 * low + 3 * side


def local_speeds(shape):
    index = lax.axis_index("vel") * shape[-1] + lax.broadcasted_iota(jnp.int32, shape, len(shape) - 1)
    along = [index // (VSIDE * VSIDE), (index // VSIDE) & (VSIDE - 1), index & (VSIDE - 1)]
    return [(entry.astype(jnp.float32) + 0.5) * (2.0 / VSIDE) - 1.0 for entry in along]


def inflow_faces(speeds):
    return [speeds[f // 2] > 0.0 if f % 2 == 0 else speeds[f // 2] < 0.0 for f in range(6)]


def inflow_masks(shape):
    ones = [jnp.where(on, 1.0, 0.0) for on in inflow_faces(local_speeds(shape))]
    return [one.astype(jnp.bfloat16) for one in ones]


def fetched(sems, *pairs):
    copies = [pltpu.make_async_copy(src, dst, sems.at[i]) for i, (src, dst) in enumerate(pairs)]
    for copy in copies:
        copy.start()
    return copies


def face_selector(nodes):
    node = lax.broadcasted_iota(jnp.int32, (16, nodes), 1)
    picks = [jnp.where(face_nodes(f, (16, nodes), 0) == node, 1.0, 0.0) for f in range(6)]
    return jnp.concatenate(picks, axis=0).astype(jnp.bfloat16)


def extract_traces(held, rows):
    elements, nodes, width = held.shape
    select = face_selector(nodes)
    for at in range(elements):
        traces = dot(select, held[at]).astype(jnp.bfloat16)
        rows[6 * at : 6 * at + 6] = traces.reshape(6, 16, width)


def send_kernel(
    faces_hbm,
    count_hbm,
    source_hbm,
    level_hbm,
    dist_hbm,
    near_ref,
    far_ref,
    held,
    rows,
    source,
    level,
    faces,
    count,
    sems,
):
    pairs = (faces_hbm, faces), (count_hbm, count), (dist_hbm, held), (source_hbm, source)
    copies = fetched(sems, *pairs, (level_hbm, level))
    for copy in copies:
        copy.wait()
    extract_traces(held, rows)
    near_way = 1 - (lax.axis_index("space") & 1)
    for way, out in ((1 - near_way, far_ref), (near_way, near_ref)):
        for slot in range(SLOTS):
            keep = jnp.where(slot < count[0, way], 1.0, 0.0).astype(jnp.bfloat16)
            out[slot] = rows[faces[0, way, slot]] * keep


def transport_kernel(
    source, level, held, rows, near_ref, far_ref, table_ref, out_ref, traces, stack
):
    elements, nodes, width = held.shape
    faces = 6 * elements
    odd = lax.axis_index("space") & 1
    traces[:faces] = rows[...]
    traces[pl.ds(faces + SLOTS * (1 - odd), SLOTS)] = near_ref[pl.ds(SLOTS * (1 - odd), SLOTS)]
    traces[pl.ds(faces + SLOTS * odd, SLOTS)] = far_ref[...]
    speeds = local_speeds((1, width))
    masks = inflow_masks((16, width))
    wide = local_speeds((nodes, width))
    node = lax.broadcasted_iota(jnp.int32, (nodes, width), 0)
    digits = [node >> 4, (node >> 2) & 3, node & 3]
    loss = jnp.zeros((nodes, width), jnp.float32)
    for face, on in enumerate(inflow_faces(wide)):
        member = jnp.logical_and(on, digits[face // 2] == 3 * (face % 2))
        loss = loss + jnp.where(member, jnp.abs(wide[face // 2]), 0.0)
    keep = 1.0 - courant * lift_weight * loss
    gradient = table_ref[30:].reshape(3 * nodes, table_ref.shape[2])[:, :nodes]
    for at in range(elements):
        for face in range(6):
            trace = traces[source[face, at]] * masks[face]
            stack[at, 16 * face : 16 * face + 16] = trace
        stack[at, 96:] = jnp.zeros((32, width), jnp.bfloat16)
        left = jnp.concatenate(
            [
                table_ref[10 * axis + level[2 * axis, at]]
                + table_ref[10 * axis + 5 + level[2 * axis + 1, at]]
                for axis in range(3)
            ],
            axis=0,
        )
        moved = dot(gradient, held[at])
        lifted = dot(left, stack[at])
        total = held[at].astype(jnp.float32) * keep
        for axis in range(3):
            part = slice(64 * axis, 64 * axis + 64)
            total = total + moved[part] * (-courant * speeds[axis])
            total = total + lifted[part] * (-courant * lift_weight * speeds[axis])
        out_ref[at] = total.astype(jnp.bfloat16)


def collide_kernel(dist_ref, alpha_ref, beta_ref, into_ref, back_ref, out_ref):
    nodes, plane = dist_ref.shape[1], dist_ref.shape[2]
    modes = alpha_ref.shape[0]

    def planes(array):
        cube = array.reshape(VSIDE, GROUP, plane)
        return [cube[i] for i in range(VSIDE)]

    for start in range(0, nodes, GROUP):
        group = slice(start, start + GROUP)
        values = dist_ref[:, group, :].reshape(VSIDE * GROUP, plane)
        spectrum = cosine_forward(planes(dot(values, into_ref[0]) + dot(values, into_ref[1])))
        spectrum[0] = 0.5 * spectrum[0]

        def field(kern, row):
            parts = [
                (spectrum[i] * kern[row : row + 1, i * plane : (i + 1) * plane]).astype(jnp.bfloat16)
                for i in range(VSIDE)
            ]
            left = jnp.concatenate(parts, axis=0)
            return cosine_backward(planes(dot(left, back_ref[0]) + dot(left, back_ref[1])))

        gain = None
        for mode in range(modes):
            pairs = zip(field(alpha_ref, mode), field(beta_ref, mode))
            products = [first * second for first, second in pairs]
            gain = products if mode == 0 else [a + b for a, b in zip(gain, products)]
        loss = field(beta_ref, modes)
        for i in range(VSIDE):
            value = dist_ref[i, group, :].astype(jnp.float32)
            total = value + relax_step * (gain[i] - value * loss[i])
            out_ref[i, group, :] = total.astype(jnp.bfloat16)


def in_vmem():
    return pl.BlockSpec(memory_space=pltpu.VMEM)


def in_hbm():
    return pl.BlockSpec(memory_space=pltpu.HBM)


def in_smem():
    return pl.BlockSpec(memory_space=pltpu.SMEM)


def on_chip(*arrays):
    return [pltpu.with_memory_space_constraint(array, pltpu.VMEM) for array in arrays]


def in_scalar(*arrays):
    return [pltpu.with_memory_space_constraint(array, pltpu.SMEM) for array in arrays]


def off_chip(*arrays):
    return [pltpu.with_memory_space_constraint(array, pltpu.HBM) for array in arrays]


def on_device(dist, send_faces, send_count, source_face, subface, alpha, beta):
    elements, nodes, width = dist.shape
    faces = 6 * elements
    traces = pltpu.VMEM((SLOTS, 16, width), jnp.bfloat16)
    block = pltpu.VMEM(dist.shape, jnp.bfloat16)

    sources, levels = source_face.T, subface.T
    indices = pltpu.SMEM(sources.shape, jnp.int32)
    near, far, held, rows, source, level = pl.pallas_call(
        send_kernel,
        out_shape=(
            traces,
            traces,
            block,
            pltpu.VMEM((faces, 16, width), jnp.bfloat16),
            indices,
            indices,
        ),
        in_specs=[in_hbm()] * 5,
        out_specs=(in_vmem(),) * 4 + (in_smem(),) * 2,
        scratch_shapes=[
            pltpu.SMEM(send_faces.shape, jnp.int32),
            pltpu.SMEM(send_count.shape, jnp.int32),
            pltpu.SemaphoreType.DMA((5,)),
        ],
        compiler_params=pltpu.CompilerParams(vmem_limit_bytes=SCOPED),
        name="send_traces",
    )(*off_chip(send_faces, send_count, sources, levels, dist))
    blocks = lax.axis_size("space")
    across = [((i + 1) % blocks, ((i ^ 1) + 1) % blocks) for i in range(blocks)]
    far = lax.ppermute(far, "space", across)
    couples = [[i, i + 1] for i in range(0, blocks, 2)]
    near = lax.all_gather(near, "space", axis=0, tiled=True, axis_index_groups=couples)

    updated = pl.pallas_call(
        transport_kernel,
        out_shape=block,
        in_specs=[in_smem()] * 2 + [in_vmem()] * 5,
        out_specs=in_vmem(),
        scratch_shapes=[
            pltpu.VMEM((faces + 2 * SLOTS, 16, width), jnp.bfloat16),
            pltpu.VMEM((elements, 128, width), jnp.bfloat16),
        ],
        compiler_params=pltpu.CompilerParams(vmem_limit_bytes=SCOPED),
        name="transport",
    )(
        *in_scalar(source, level),
        *on_chip(held, rows, near, far, jnp.asarray(transport_tables())),
    )

    plane = VSIDE * VSIDE
    cosine = cosine_table()
    pair = np.kron(cosine, cosine)
    into = jnp.asarray(np.stack(split_table(pair.T * (2.0 / VSIDE))))
    out_of = jnp.asarray(np.stack(split_table(pair)))
    whole = lax.all_to_all(updated, "vel", split_axis=0, concat_axis=0, tiled=True)
    mixed = pl.pallas_call(
        collide_kernel,
        out_shape=pltpu.VMEM(whole.shape, jnp.bfloat16),
        in_specs=[in_vmem()] * 5,
        out_specs=in_vmem(),
        compiler_params=pltpu.CompilerParams(vmem_limit_bytes=SCOPED),
        name="collide",
    )(*on_chip(whole, alpha, beta, into, out_of))
    return lax.all_to_all(mixed, "vel", split_axis=0, concat_axis=0, tiled=True)


def solution(mesh):
    return jax.shard_map(
        on_device,
        mesh=mesh,
        in_specs=(
            P("space", None, "vel"),
            P("space", None, None),
            P("space", None),
            P("space", None),
            P("space", None),
            P(),
            P(),
        ),
        out_specs=P("space", None, "vel"),
        check_vma=False,
    )
```

```python
import jax
import jax.numpy as jnp
import ml_dtypes
import numpy as np
from jax import lax
from jax.experimental import pallas as pl
from jax.experimental.pallas import tpu as pltpu
from jax.sharding import PartitionSpec as P

VSIDE = 16
SLOTS = 16
GROUP = 16
AHEAD = 3
SCOPED = 16 << 20


courant = 0.1
lift_weight = 6.0
relax_step = 0.5


def passed_along(block, axis, distance):
    devices = range(lax.axis_size(axis))
    route = [((i - distance) % len(devices), i) for i in devices]
    return lax.ppermute(block, axis, route)


def lobatto_points():
    return np.array([-1.0, -1.0 / np.sqrt(5.0), 1.0 / np.sqrt(5.0), 1.0])


def lagrange_table(targets):
    points = lobatto_points()
    result = np.ones((targets.shape[0], 4))
    for column in range(4):
        for second in range(4):
            if second != column:
                result[:, column] = (
                    result[:, column]
                    * (targets - points[second])
                    / (points[column] - points[second])
                )
    return result


def derivative_table():
    points = lobatto_points()
    result = np.zeros((4, 4))
    for row_at in range(4):
        for column in range(4):
            total = 0.0
            for skipped in range(4):
                if skipped != column:
                    factor = 1.0 / (points[column] - points[skipped])
                    for second in range(4):
                        if second != column and second != skipped:
                            factor = (
                                factor
                                * (points[row_at] - points[second])
                                / (points[column] - points[second])
                            )
                    total = total + factor
            result[row_at, column] = total
    return result


def cosine_table():
    index_list = np.arange(VSIDE)
    result = np.sqrt(2.0 / VSIDE) * np.cos(
        np.pi * (index_list[None, :] + 0.5) * index_list[:, None] / VSIDE
    )
    result[0] = result[0] / np.sqrt(2.0)
    return result


def static_tables():
    derivative = derivative_table()
    eye_four = np.eye(4)
    gradients = np.stack(
        [
            np.kron(np.kron(derivative, eye_four), eye_four),
            np.kron(np.kron(eye_four, derivative), eye_four),
            np.kron(np.kron(eye_four, eye_four), derivative),
        ]
    )
    selector = np.zeros((96, 64))
    for axis_at in range(3):
        for side_at in range(2):
            filled = 0
            for node_at in range(64):
                digits = (node_at // 16, node_at // 4 % 4, node_at % 4)
                if digits[axis_at] == 3 * side_at:
                    selector[(2 * axis_at + side_at) * 16 + filled, node_at] = 1.0
                    filled = filled + 1
    points = lobatto_points()
    halves = [lagrange_table((points - 1.0) / 2.0), lagrange_table((points + 1.0) / 2.0)]
    mortar = np.stack(
        [np.eye(16)]
        + [np.kron(halves[(which - 1) // 2], halves[(which - 1) % 2]) for which in range(1, 5)]
    )
    return (gradients, selector, mortar)


def split_table(table):
    high = np.asarray(table, np.float32).astype(ml_dtypes.bfloat16)
    rest = np.asarray(table, np.float64) - high.astype(np.float64)
    return (high, np.asarray(rest, np.float32).astype(ml_dtypes.bfloat16))


def transport_tables():
    gradients, selector, mortar = static_tables()
    tables = np.zeros((33, 64, 128))
    for face in range(6):
        lift = selector[face * 16 : face * 16 + 16].T
        sign = -1.0 if face % 2 == 0 else 1.0
        for level in range(5):
            placed = sign * (lift @ mortar[level])
            tables[5 * face + level, :, face * 16 : face * 16 + 16] = placed
    tables[30:, :, :64] = gradients
    return tables.astype(np.float32).astype(ml_dtypes.bfloat16)


def cosine_forward(values):
    count = len(values)
    if count == 1:
        return values
    half = count // 2
    sums = [values[i] + values[count - 1 - i] for i in range(half)]
    gaps = [
        (values[i] - values[count - 1 - i]) * float(0.5 / np.cos((i + 0.5) * np.pi / count))
        for i in range(half)
    ]
    even, odd = cosine_forward(sums), cosine_forward(gaps)
    result = []
    for i in range(half):
        result.append(even[i])
        result.append(odd[i] + odd[i + 1] if i + 1 < half else odd[i])
    return result


def cosine_backward(values):
    count = len(values)
    if count == 1:
        return values
    half = count // 2
    even = [values[2 * i] for i in range(half)]
    odd = [values[1]] + [values[2 * i - 1] + values[2 * i + 1] for i in range(1, half)]
    sums, gaps = cosine_backward(even), cosine_backward(odd)
    scaled = [gaps[i] * float(0.5 / np.cos((i + 0.5) * np.pi / count)) for i in range(half)]
    return [sums[i] + scaled[i] for i in range(half)] + [
        sums[half - 1 - i] - scaled[half - 1 - i] for i in range(half)
    ]


def dot(left, right):
    return jnp.dot(left, right, preferred_element_type=jnp.float32)


def face_nodes(face, shape, along):
    at = lax.broadcasted_iota(jnp.int32, shape, along)
    axis, side = face // 2, face % 2
    if axis == 0:
        return at + 48 * side
    high, low = at >> 2, at & 3
    return 16 * high + 12 * side + low if axis == 1 else 16 * high + 4 * low + 3 * side


def local_speeds(shape):
    index = lax.axis_index("vel") * shape[-1] + lax.broadcasted_iota(jnp.int32, shape, len(shape) - 1)
    along = [index // (VSIDE * VSIDE), (index // VSIDE) & (VSIDE - 1), index & (VSIDE - 1)]
    return [(entry.astype(jnp.float32) + 0.5) * (2.0 / VSIDE) - 1.0 for entry in along]


def inflow_faces(speeds):
    return [speeds[f // 2] > 0.0 if f % 2 == 0 else speeds[f // 2] < 0.0 for f in range(6)]


def inflow_masks(shape):
    ones = [jnp.where(on, 1.0, 0.0) for on in inflow_faces(local_speeds(shape))]
    return [one.astype(jnp.bfloat16) for one in ones]


def fetched(sems, *pairs):
    copies = [pltpu.make_async_copy(src, dst, sems.at[i]) for i, (src, dst) in enumerate(pairs)]
    for copy in copies:
        copy.start()
    return copies


def face_selector(nodes):
    node = lax.broadcasted_iota(jnp.int32, (16, nodes), 1)
    picks = [jnp.where(face_nodes(f, (16, nodes), 0) == node, 1.0, 0.0) for f in range(6)]
    return jnp.concatenate(picks, axis=0).astype(jnp.bfloat16)


def extract_traces(held, rows):
    elements, nodes, width = held.shape
    select = face_selector(nodes)
    for at in range(elements):
        traces = dot(select, held[at]).astype(jnp.bfloat16)
        rows[6 * at : 6 * at + 6] = traces.reshape(6, 16, width)


def send_kernel(
    faces_hbm,
    count_hbm,
    source_hbm,
    level_hbm,
    dist_hbm,
    back_ref,
    ahead_ref,
    held,
    source,
    level,
    picks,
    faces,
    count,
    sems,
):
    pairs = (faces_hbm, faces), (count_hbm, count), (dist_hbm, held), (source_hbm, source)
    copies = fetched(sems, *pairs, (level_hbm, level))
    picks[...] = face_selector(held.shape[1]).reshape(picks.shape)
    for copy in copies:
        copy.wait()
    for way, out in enumerate((back_ref, ahead_ref)):
        for slot in range(SLOTS):
            keep = jnp.where(slot < count[0, way], 1.0, 0.0).astype(jnp.bfloat16)
            number = faces[0, way, slot]
            element = number // 6
            trace = dot(picks[number - 6 * element], held[element])
            out[slot] = trace.astype(jnp.bfloat16) * keep


def add_lifts(left, stacked, total):
    speeds = local_speeds((1, total.shape[-1]))
    lifted = dot(left, stacked)
    for axis in range(3):
        weight = -courant * lift_weight * speeds[axis]
        total = total + lifted[64 * axis : 64 * axis + 64] * weight
    return total


def local_kernel(source, level, held, table_ref, out_ref, left_ref, rows, stack):
    elements, nodes, width = held.shape
    faces = 6 * elements
    speeds = local_speeds((1, width))
    masks = inflow_masks((16, width))
    wide = local_speeds((nodes, width))
    node = lax.broadcasted_iota(jnp.int32, (nodes, width), 0)
    digits = [node >> 4, (node >> 2) & 3, node & 3]
    loss = jnp.zeros((nodes, width), jnp.float32)
    for face, on in enumerate(inflow_faces(wide)):
        member = jnp.logical_and(on, digits[face // 2] == 3 * (face % 2))
        loss = loss + jnp.where(member, jnp.abs(wide[face // 2]), 0.0)
    keep = 1.0 - courant * lift_weight * loss
    extract_traces(held, rows)
    rows[faces] = jnp.zeros((16, width), jnp.bfloat16)
    gradient = table_ref[30:].reshape(3 * nodes, table_ref.shape[2])[:, :nodes]
    for at in range(elements):
        for face in range(6):
            trace = rows[jnp.minimum(source[face, at], faces)] * masks[face]
            stack[at, 16 * face : 16 * face + 16] = trace
        stack[at, 96:] = jnp.zeros((32, width), jnp.bfloat16)
        total = held[at].astype(jnp.float32) * keep
        moved = dot(gradient, held[at])
        for axis in range(3):
            total = total + moved[64 * axis : 64 * axis + 64] * (-courant * speeds[axis])
        left = jnp.concatenate(
            [
                table_ref[10 * axis + level[2 * axis, at]]
                + table_ref[10 * axis + 5 + level[2 * axis + 1, at]]
                for axis in range(3)
            ],
            axis=0,
        )
        left_ref[at] = left
        out_ref[at] = add_lifts(left, stack[at], total)


def remote_kernel(source, part_ref, left_ref, prev_ref, next_ref, out_ref, table, stack):
    elements, _, width = part_ref.shape
    faces = 6 * elements
    table[0] = jnp.zeros((16, width), jnp.bfloat16)
    table[1 : SLOTS + 1] = prev_ref[...]
    table[SLOTS + 1 :] = next_ref[...]
    masks = inflow_masks((16, width))
    for at in range(elements):
        for face in range(6):
            trace = table[jnp.maximum(source[face, at] - (faces - 1), 0)] * masks[face]
            stack[at, 16 * face : 16 * face + 16] = trace
        stack[at, 96:] = jnp.zeros((32, width), jnp.bfloat16)
        out_ref[at] = add_lifts(left_ref[at], stack[at], part_ref[at]).astype(jnp.bfloat16)


def collide_kernel(dist_ref, alpha_ref, beta_ref, into_ref, back_ref, out_ref):
    nodes, plane = dist_ref.shape[1], dist_ref.shape[2]
    modes = alpha_ref.shape[0]

    def planes(array):
        cube = array.reshape(VSIDE, GROUP, plane)
        return [cube[i] for i in range(VSIDE)]

    order = [(kern, mode) for mode in range(modes) for kern in (alpha_ref, beta_ref)]
    order.append((beta_ref, modes))

    def gathered(start, ahead):
        group = slice(start, start + GROUP)
        values = dist_ref[:, group, :].reshape(VSIDE * GROUP, plane)
        spectrum = cosine_forward(planes(dot(values, into_ref[0]) + dot(values, into_ref[1])))
        spectrum[0] = 0.5 * spectrum[0]
        pending = []
        for at in range(len(order) + ahead):
            if at < len(order):
                kern, row = order[at]
                parts = [
                    spectrum[i] * kern[row : row + 1, i * plane : (i + 1) * plane]
                    for i in range(VSIDE)
                ]
                left = jnp.concatenate([part.astype(jnp.bfloat16) for part in parts], axis=0)
                pending.append(dot(left, back_ref[0]) + dot(left, back_ref[1]))
            if at >= ahead:
                yield cosine_backward(planes(pending.pop(0)))

    for start in range(0, nodes, GROUP):
        group = slice(start, start + GROUP)
        gain, first = None, None
        for at, field in enumerate(gathered(start, AHEAD)):
            if at == 2 * modes:
                for i in range(VSIDE):
                    value = dist_ref[i, group, :].astype(jnp.float32)
                    total = value + relax_step * (gain[i] - value * field[i])
                    out_ref[i, group, :] = total.astype(jnp.bfloat16)
            elif at % 2 == 0:
                first = field
            else:
                products = [a * b for a, b in zip(first, field)]
                gain = products if at == 1 else [a + b for a, b in zip(gain, products)]


def in_vmem():
    return pl.BlockSpec(memory_space=pltpu.VMEM)


def in_hbm():
    return pl.BlockSpec(memory_space=pltpu.HBM)


def in_smem():
    return pl.BlockSpec(memory_space=pltpu.SMEM)


def on_chip(*arrays):
    return [pltpu.with_memory_space_constraint(array, pltpu.VMEM) for array in arrays]


def in_scalar(*arrays):
    return [pltpu.with_memory_space_constraint(array, pltpu.SMEM) for array in arrays]


def off_chip(*arrays):
    return [pltpu.with_memory_space_constraint(array, pltpu.HBM) for array in arrays]


def on_device(dist, send_faces, send_count, source_face, subface, alpha, beta):
    elements, nodes, width = dist.shape
    faces = 6 * elements
    traces = pltpu.VMEM((SLOTS, 16, width), jnp.bfloat16)
    block = pltpu.VMEM(dist.shape, jnp.bfloat16)

    sources, levels = source_face.T, subface.T
    indices = pltpu.SMEM(sources.shape, jnp.int32)
    back, ahead, held, source, level = pl.pallas_call(
        send_kernel,
        out_shape=(
            traces,
            traces,
            block,
            indices,
            indices,
        ),
        in_specs=[in_hbm()] * 5,
        out_specs=(in_vmem(),) * 3 + (in_smem(),) * 2,
        scratch_shapes=[
            pltpu.VMEM((6, 16, nodes), jnp.bfloat16),
            pltpu.SMEM(send_faces.shape, jnp.int32),
            pltpu.SMEM(send_count.shape, jnp.int32),
            pltpu.SemaphoreType.DMA((5,)),
        ],
        compiler_params=pltpu.CompilerParams(vmem_limit_bytes=SCOPED),
        name="send_traces",
    )(*off_chip(send_faces, send_count, sources, levels, dist))
    from_prev = passed_along(ahead, "space", 1)
    from_next = passed_along(back, "space", -1)

    source, level = in_scalar(source, level)
    part, left = pl.pallas_call(
        local_kernel,
        out_shape=(
            pltpu.VMEM(dist.shape, jnp.float32),
            pltpu.VMEM((elements, 3 * nodes, 128), jnp.bfloat16),
        ),
        in_specs=[in_smem()] * 2 + [in_vmem()] * 2,
        out_specs=(in_vmem(), in_vmem()),
        scratch_shapes=[
            pltpu.VMEM((faces + 1, 16, width), jnp.bfloat16),
            pltpu.VMEM((elements, 128, width), jnp.bfloat16),
        ],
        compiler_params=pltpu.CompilerParams(vmem_limit_bytes=SCOPED),
        name="transport_local",
    )(source, level, *on_chip(held, jnp.asarray(transport_tables())))
    updated = pl.pallas_call(
        remote_kernel,
        out_shape=block,
        in_specs=[in_smem()] + [in_vmem()] * 4,
        out_specs=in_vmem(),
        scratch_shapes=[
            pltpu.VMEM((2 * SLOTS + 1, 16, width), jnp.bfloat16),
            pltpu.VMEM((elements, 128, width), jnp.bfloat16),
        ],
        compiler_params=pltpu.CompilerParams(vmem_limit_bytes=SCOPED),
        name="transport_remote",
    )(source, *on_chip(part, left, from_prev, from_next))

    plane = VSIDE * VSIDE
    cosine = cosine_table()
    pair = np.kron(cosine, cosine)
    into = jnp.asarray(np.stack(split_table(pair.T * (2.0 / VSIDE))))
    out_of = jnp.asarray(np.stack(split_table(pair)))
    whole = lax.all_to_all(updated, "vel", split_axis=0, concat_axis=0, tiled=True)
    mixed = pl.pallas_call(
        collide_kernel,
        out_shape=pltpu.VMEM(whole.shape, jnp.bfloat16),
        in_specs=[in_vmem()] * 5,
        out_specs=in_vmem(),
        compiler_params=pltpu.CompilerParams(vmem_limit_bytes=SCOPED),
        name="collide",
    )(*on_chip(whole, alpha, beta, into, out_of))
    return lax.all_to_all(mixed, "vel", split_axis=0, concat_axis=0, tiled=True)


def solution(mesh):
    return jax.shard_map(
        on_device,
        mesh=mesh,
        in_specs=(
            P("space", None, "vel"),
            P("space", None, None),
            P("space", None),
            P("space", None),
            P("space", None),
            P(),
            P(),
        ),
        out_specs=P("space", None, "vel"),
        check_vma=False,
    )
```

```python
import jax
import jax.numpy as jnp
import ml_dtypes
import numpy as np
from jax import lax
from jax.experimental import pallas as pl
from jax.experimental.pallas import tpu as pltpu
from jax.sharding import PartitionSpec as P

VSIDE = 16
SLOTS = 16
GROUP = 16
AHEAD = 3
SCOPED = 16 << 20


courant = 0.1
lift_weight = 6.0
relax_step = 0.5


def passed_along(block, axis, distance):
    devices = range(lax.axis_size(axis))
    route = [((i - distance) % len(devices), i) for i in devices]
    return lax.ppermute(block, axis, route)


def lobatto_points():
    return np.array([-1.0, -1.0 / np.sqrt(5.0), 1.0 / np.sqrt(5.0), 1.0])


def lagrange_table(targets):
    points = lobatto_points()
    result = np.ones((targets.shape[0], 4))
    for column in range(4):
        for second in range(4):
            if second != column:
                result[:, column] = (
                    result[:, column]
                    * (targets - points[second])
                    / (points[column] - points[second])
                )
    return result


def derivative_table():
    points = lobatto_points()
    result = np.zeros((4, 4))
    for row_at in range(4):
        for column in range(4):
            total = 0.0
            for skipped in range(4):
                if skipped != column:
                    factor = 1.0 / (points[column] - points[skipped])
                    for second in range(4):
                        if second != column and second != skipped:
                            factor = (
                                factor
                                * (points[row_at] - points[second])
                                / (points[column] - points[second])
                            )
                    total = total + factor
            result[row_at, column] = total
    return result


def cosine_table():
    index_list = np.arange(VSIDE)
    result = np.sqrt(2.0 / VSIDE) * np.cos(
        np.pi * (index_list[None, :] + 0.5) * index_list[:, None] / VSIDE
    )
    result[0] = result[0] / np.sqrt(2.0)
    return result


def static_tables():
    derivative = derivative_table()
    eye_four = np.eye(4)
    gradients = np.stack(
        [
            np.kron(np.kron(derivative, eye_four), eye_four),
            np.kron(np.kron(eye_four, derivative), eye_four),
            np.kron(np.kron(eye_four, eye_four), derivative),
        ]
    )
    selector = np.zeros((96, 64))
    for axis_at in range(3):
        for side_at in range(2):
            filled = 0
            for node_at in range(64):
                digits = (node_at // 16, node_at // 4 % 4, node_at % 4)
                if digits[axis_at] == 3 * side_at:
                    selector[(2 * axis_at + side_at) * 16 + filled, node_at] = 1.0
                    filled = filled + 1
    points = lobatto_points()
    halves = [lagrange_table((points - 1.0) / 2.0), lagrange_table((points + 1.0) / 2.0)]
    mortar = np.stack(
        [np.eye(16)]
        + [np.kron(halves[(which - 1) // 2], halves[(which - 1) % 2]) for which in range(1, 5)]
    )
    return (gradients, selector, mortar)


def split_table(table):
    high = np.asarray(table, np.float32).astype(ml_dtypes.bfloat16)
    rest = np.asarray(table, np.float64) - high.astype(np.float64)
    return (high, np.asarray(rest, np.float32).astype(ml_dtypes.bfloat16))


def transport_tables():
    gradients, selector, mortar = static_tables()
    tables = np.zeros((33, 64, 128))
    for face in range(6):
        lift = selector[face * 16 : face * 16 + 16].T
        sign = -1.0 if face % 2 == 0 else 1.0
        for level in range(5):
            placed = sign * (lift @ mortar[level])
            tables[5 * face + level, :, face * 16 : face * 16 + 16] = placed
    tables[30:, :, :64] = gradients
    return tables.astype(np.float32).astype(ml_dtypes.bfloat16)


def cosine_forward(values):
    count = len(values)
    if count == 1:
        return values
    half = count // 2
    sums = [values[i] + values[count - 1 - i] for i in range(half)]
    gaps = [
        (values[i] - values[count - 1 - i]) * float(0.5 / np.cos((i + 0.5) * np.pi / count))
        for i in range(half)
    ]
    even, odd = cosine_forward(sums), cosine_forward(gaps)
    result = []
    for i in range(half):
        result.append(even[i])
        result.append(odd[i] + odd[i + 1] if i + 1 < half else odd[i])
    return result


def cosine_backward(values):
    count = len(values)
    if count == 1:
        return values
    half = count // 2
    even = [values[2 * i] for i in range(half)]
    odd = [values[1]] + [values[2 * i - 1] + values[2 * i + 1] for i in range(1, half)]
    sums, gaps = cosine_backward(even), cosine_backward(odd)
    scaled = [gaps[i] * float(0.5 / np.cos((i + 0.5) * np.pi / count)) for i in range(half)]
    return [sums[i] + scaled[i] for i in range(half)] + [
        sums[half - 1 - i] - scaled[half - 1 - i] for i in range(half)
    ]


def dot(left, right):
    return jnp.dot(left, right, preferred_element_type=jnp.float32)


def face_nodes(face, shape, along):
    at = lax.broadcasted_iota(jnp.int32, shape, along)
    axis, side = face // 2, face % 2
    if axis == 0:
        return at + 48 * side
    high, low = at >> 2, at & 3
    return 16 * high + 12 * side + low if axis == 1 else 16 * high + 4 * low + 3 * side


def local_speeds(shape):
    index = lax.axis_index("vel") * shape[-1] + lax.broadcasted_iota(jnp.int32, shape, len(shape) - 1)
    along = [index // (VSIDE * VSIDE), (index // VSIDE) & (VSIDE - 1), index & (VSIDE - 1)]
    return [(entry.astype(jnp.float32) + 0.5) * (2.0 / VSIDE) - 1.0 for entry in along]


def inflow_faces(speeds):
    return [speeds[f // 2] > 0.0 if f % 2 == 0 else speeds[f // 2] < 0.0 for f in range(6)]


def inflow_masks(shape):
    ones = [jnp.where(on, 1.0, 0.0) for on in inflow_faces(local_speeds(shape))]
    return [one.astype(jnp.bfloat16) for one in ones]


def fetched(sems, *pairs):
    copies = [pltpu.make_async_copy(src, dst, sems.at[i]) for i, (src, dst) in enumerate(pairs)]
    for copy in copies:
        copy.start()
    return copies


def face_selector(nodes):
    node = lax.broadcasted_iota(jnp.int32, (16, nodes), 1)
    picks = [jnp.where(face_nodes(f, (16, nodes), 0) == node, 1.0, 0.0) for f in range(6)]
    return jnp.concatenate(picks, axis=0).astype(jnp.bfloat16)


def extract_traces(held, rows):
    elements, nodes, width = held.shape
    select = face_selector(nodes)
    for at in range(elements):
        traces = dot(select, held[at]).astype(jnp.bfloat16)
        rows[6 * at : 6 * at + 6] = traces.reshape(6, 16, width)


def send_kernel(
    faces_hbm,
    count_hbm,
    source_hbm,
    level_hbm,
    dist_hbm,
    back_ref,
    ahead_ref,
    held,
    source,
    level,
    picks,
    faces,
    count,
    sems,
):
    pairs = (dist_hbm, held), (faces_hbm, faces), (count_hbm, count), (source_hbm, source)
    copies = fetched(sems, *pairs, (level_hbm, level))
    picks[...] = face_selector(held.shape[1]).reshape(picks.shape)
    for copy in copies:
        copy.wait()
    for way, out in enumerate((back_ref, ahead_ref)):
        for slot in range(SLOTS):
            keep = jnp.where(slot < count[0, way], 1.0, 0.0).astype(jnp.bfloat16)
            number = faces[0, way, slot]
            element = number // 6
            trace = dot(picks[number - 6 * element], held[element])
            out[slot] = trace.astype(jnp.bfloat16) * keep


def add_lifts(left, stacked, total):
    speeds = local_speeds((1, total.shape[-1]))
    lifted = dot(left, stacked)
    for axis in range(3):
        weight = -courant * lift_weight * speeds[axis]
        total = total + lifted[64 * axis : 64 * axis + 64] * weight
    return total


def local_kernel(source, level, held, table_ref, out_ref, left_ref, rows, stack):
    elements, nodes, width = held.shape
    faces = 6 * elements
    speeds = local_speeds((1, width))
    masks = inflow_masks((16, width))
    wide = local_speeds((nodes, width))
    node = lax.broadcasted_iota(jnp.int32, (nodes, width), 0)
    digits = [node >> 4, (node >> 2) & 3, node & 3]
    loss = jnp.zeros((nodes, width), jnp.float32)
    for face, on in enumerate(inflow_faces(wide)):
        member = jnp.logical_and(on, digits[face // 2] == 3 * (face % 2))
        loss = loss + jnp.where(member, jnp.abs(wide[face // 2]), 0.0)
    keep = 1.0 - courant * lift_weight * loss
    extract_traces(held, rows)
    rows[faces] = jnp.zeros((16, width), jnp.bfloat16)
    gradient = table_ref[30:].reshape(3 * nodes, table_ref.shape[2])[:, :nodes]
    for at in range(elements):
        for face in range(6):
            trace = rows[jnp.minimum(source[face, at], faces)] * masks[face]
            stack[at, 16 * face : 16 * face + 16] = trace
        stack[at, 96:] = jnp.zeros((32, width), jnp.bfloat16)
        total = held[at].astype(jnp.float32) * keep
        moved = dot(gradient, held[at])
        for axis in range(3):
            total = total + moved[64 * axis : 64 * axis + 64] * (-courant * speeds[axis])
        left = jnp.concatenate(
            [
                table_ref[10 * axis + level[2 * axis, at]]
                + table_ref[10 * axis + 5 + level[2 * axis + 1, at]]
                for axis in range(3)
            ],
            axis=0,
        )
        left_ref[at] = left
        out_ref[at] = add_lifts(left, stack[at], total)


def remote_kernel(source, part_ref, left_ref, prev_ref, next_ref, out_ref, table, stack):
    elements, _, width = part_ref.shape
    faces = 6 * elements
    table[0] = jnp.zeros((16, width), jnp.bfloat16)
    table[1 : SLOTS + 1] = prev_ref[...]
    table[SLOTS + 1 :] = next_ref[...]
    masks = inflow_masks((16, width))
    for at in range(elements):
        for face in range(6):
            trace = table[jnp.maximum(source[face, at] - (faces - 1), 0)] * masks[face]
            stack[at, 16 * face : 16 * face + 16] = trace
        stack[at, 96:] = jnp.zeros((32, width), jnp.bfloat16)
        out_ref[at] = add_lifts(left_ref[at], stack[at], part_ref[at]).astype(jnp.bfloat16)


def collide_kernel(dist_ref, alpha_ref, beta_ref, into_ref, back_ref, out_ref):
    nodes, plane = dist_ref.shape[1], dist_ref.shape[2]
    modes = alpha_ref.shape[0]

    def planes(array):
        cube = array.reshape(VSIDE, GROUP, plane)
        return [cube[i] for i in range(VSIDE)]

    order = [(kern, mode) for mode in range(modes) for kern in (alpha_ref, beta_ref)]
    order.append((beta_ref, modes))

    def gathered(start, ahead):
        group = slice(start, start + GROUP)
        values = dist_ref[:, group, :].reshape(VSIDE * GROUP, plane)
        spectrum = cosine_forward(planes(dot(values, into_ref[0]) + dot(values, into_ref[1])))
        spectrum[0] = 0.5 * spectrum[0]
        pending = []
        for at in range(len(order) + ahead):
            if at < len(order):
                kern, row = order[at]
                parts = [
                    spectrum[i] * kern[row : row + 1, i * plane : (i + 1) * plane]
                    for i in range(VSIDE)
                ]
                left = jnp.concatenate([part.astype(jnp.bfloat16) for part in parts], axis=0)
                pending.append(dot(left, back_ref[0]) + dot(left, back_ref[1]))
            if at >= ahead:
                yield cosine_backward(planes(pending.pop(0)))

    for start in range(0, nodes, GROUP):
        group = slice(start, start + GROUP)
        gain, first = None, None
        for at, field in enumerate(gathered(start, AHEAD)):
            if at == 2 * modes:
                for i in range(VSIDE):
                    value = dist_ref[i, group, :].astype(jnp.float32)
                    total = value + relax_step * (gain[i] - value * field[i])
                    out_ref[i, group, :] = total.astype(jnp.bfloat16)
            elif at % 2 == 0:
                first = field
            else:
                products = [a * b for a, b in zip(first, field)]
                gain = products if at == 1 else [a + b for a, b in zip(gain, products)]


def in_vmem():
    return pl.BlockSpec(memory_space=pltpu.VMEM)


def in_hbm():
    return pl.BlockSpec(memory_space=pltpu.HBM)


def in_smem():
    return pl.BlockSpec(memory_space=pltpu.SMEM)


def on_chip(*arrays):
    return [pltpu.with_memory_space_constraint(array, pltpu.VMEM) for array in arrays]


def in_scalar(*arrays):
    return [pltpu.with_memory_space_constraint(array, pltpu.SMEM) for array in arrays]


def off_chip(*arrays):
    return [pltpu.with_memory_space_constraint(array, pltpu.HBM) for array in arrays]


def on_device(dist, send_faces, send_count, source_face, subface, alpha, beta):
    elements, nodes, width = dist.shape
    faces = 6 * elements
    traces = pltpu.VMEM((SLOTS, 16, width), jnp.bfloat16)
    block = pltpu.VMEM(dist.shape, jnp.bfloat16)

    sources, levels = source_face.T, subface.T
    indices = pltpu.SMEM(sources.shape, jnp.int32)
    back, ahead, held, source, level = pl.pallas_call(
        send_kernel,
        out_shape=(
            traces,
            traces,
            block,
            indices,
            indices,
        ),
        in_specs=[in_hbm()] * 5,
        out_specs=(in_vmem(),) * 3 + (in_smem(),) * 2,
        scratch_shapes=[
            pltpu.VMEM((6, 16, nodes), jnp.bfloat16),
            pltpu.SMEM(send_faces.shape, jnp.int32),
            pltpu.SMEM(send_count.shape, jnp.int32),
            pltpu.SemaphoreType.DMA((5,)),
        ],
        compiler_params=pltpu.CompilerParams(vmem_limit_bytes=SCOPED),
        name="send_traces",
    )(*off_chip(send_faces, send_count, sources, levels, dist))
    from_prev = passed_along(ahead, "space", 1)
    from_next = passed_along(back, "space", -1)

    source, level = in_scalar(source, level)
    part, left = pl.pallas_call(
        local_kernel,
        out_shape=(
            pltpu.VMEM(dist.shape, jnp.float32),
            pltpu.VMEM((elements, 3 * nodes, 128), jnp.bfloat16),
        ),
        in_specs=[in_smem()] * 2 + [in_vmem()] * 2,
        out_specs=(in_vmem(), in_vmem()),
        scratch_shapes=[
            pltpu.VMEM((faces + 1, 16, width), jnp.bfloat16),
            pltpu.VMEM((elements, 128, width), jnp.bfloat16),
        ],
        compiler_params=pltpu.CompilerParams(vmem_limit_bytes=SCOPED),
        name="transport_local",
    )(source, level, *on_chip(held, jnp.asarray(transport_tables())))
    updated = pl.pallas_call(
        remote_kernel,
        out_shape=block,
        in_specs=[in_smem()] + [in_vmem()] * 4,
        out_specs=in_vmem(),
        scratch_shapes=[
            pltpu.VMEM((2 * SLOTS + 1, 16, width), jnp.bfloat16),
            pltpu.VMEM((elements, 128, width), jnp.bfloat16),
        ],
        compiler_params=pltpu.CompilerParams(vmem_limit_bytes=SCOPED),
        name="transport_remote",
    )(source, *on_chip(part, left, from_prev, from_next))

    plane = VSIDE * VSIDE
    cosine = cosine_table()
    pair = np.kron(cosine, cosine)
    into = jnp.asarray(np.stack(split_table(pair.T * (2.0 / VSIDE))))
    out_of = jnp.asarray(np.stack(split_table(pair)))
    whole = lax.all_to_all(updated, "vel", split_axis=0, concat_axis=0, tiled=True)
    mixed = pl.pallas_call(
        collide_kernel,
        out_shape=pltpu.VMEM(whole.shape, jnp.bfloat16),
        in_specs=[in_vmem()] * 5,
        out_specs=in_vmem(),
        compiler_params=pltpu.CompilerParams(vmem_limit_bytes=SCOPED),
        name="collide",
    )(*on_chip(whole, alpha, beta, into, out_of))
    return lax.all_to_all(mixed, "vel", split_axis=0, concat_axis=0, tiled=True)


def solution(mesh):
    return jax.shard_map(
        on_device,
        mesh=mesh,
        in_specs=(
            P("space", None, "vel"),
            P("space", None, None),
            P("space", None),
            P("space", None),
            P("space", None),
            P(),
            P(),
        ),
        out_specs=P("space", None, "vel"),
        check_vma=False,
    )
```
